32 devices in a mesh: groups: 2 (over x), blk: 8 (over z, y), rows: 2 (over core).
Axes of the slice: x: 2, y: 2, z: 4, core: 2. Of those that a mesh axis runs over, the one named last changes fastest.
Arguments:
- queries: bfloat16 [256, 2048], P(('groups', 'blk'), 'rows'), parts along dimension 0, may hold values from -170 to 170
- cache_keys: bfloat16 [8192, 256], P(('groups', 'blk'), 'rows'), parts along dimension 0, may hold values from -6 to 6
- cache_values: bfloat16 [8192, 256], P(('groups', 'blk'), 'rows'), parts along dimension 0, may hold values from -6 to 6
- span_starts: int32 [4], P('groups'), parts along dimension 0, may hold values from 0 to 4032, as said below
- out_weight: bfloat16 [2048, 2048], P(('rows', 'blk')), may hold values from -0.125 to 0.125
- norm_gain: bfloat16 [2048], replicated, may hold values from 0.099609375 to 1.8984375
- expert_ids: int32 [256, 8], P(('groups', 'blk', 'rows')), parts along dimension 0, may hold values from 0 to 15, all different within a row; in each aligned block of 8 rows (0 to 7, 8 to 15, ...) at most 8 rows name the same one
- gate_fixed: int32 [256, 8], P(('groups', 'blk', 'rows')), parts along dimension 0, may hold values from 1 to 4095
- gate_weight: bfloat16 [16, 2048, 768], P(('blk', 'rows')), may hold values from -0.125 to 0.125
- up_weight: bfloat16 [16, 2048, 768], P(('blk', 'rows')), may hold values from -0.125 to 0.125
- down_weight: bfloat16 [16, 768, 2048], P(('blk', 'rows')), may hold values from -0.21875 to 0.21875
Outputs:
- attn_proj: bfloat16 [256, 2048], P(('groups', 'blk', 'rows')), parts along dimension 0
- expert_out: bfloat16 [256, 2048], P(('groups', 'blk', 'rows')), parts along dimension 0
The draws below stay inside these ranges and needn't reach their ends.
There are 2 independent parts, one for each index of `groups`. The reference program is written for one: setup_inputs(seed, part) draws one part's arguments, and reference() takes and returns one part's arrays. A program takes and returns all parts, laid end to end along the dimension named above; an argument that names none is the same for every part. Nothing has to cross between parts.
Inputs may be any that keep to these rules, and one draw needn't show every extreme that they name: `span_starts`: the last span ends at the last cached position, entry 1 is 4032; entry 0 is at most 3968. `expert_ids`: each token names 8 different experts; among the tokens of one device (aligned blocks of 8 rows) no expert is named more than 8 times.
All inputs are finite; a program needn't handle non-finite values.
Results may differ from the reference program's by a relative error of at most 0.035.
Values may be sent and summed in bfloat16 or wider, within the bound.
No kernel may reach another device: no remote copies, remote signals or barrier semaphores. Data moves between devices by JAX's collectives and lax.ppermute only.
A program may use at most 64 MiB of HBM per device.

```python
import math
import jax
import jax.numpy as jnp
import numpy as np
from jax import lax

D = 2048
QH = 16
KVH = 2
HD = 128
FF_E = 768
TOP = 8
CACHE_DEV = 512
QTOK = 128
SPAN_LEN = 64
CACHE = 4096
MOE_TOK = 8
EXPERTS = 16
CAP = 8
N_BLK = 8


def spike_plan(key):
    base_keys = jax.random.normal(jax.random.fold_in(key, 101), (CACHE, KVH * HD), jnp.float32)
    base_keys = jnp.clip(base_keys, -6.0, 6.0)
    return base_keys


def draw_cache_keys(key, part):
    base_keys = spike_plan(key)
    return base_keys.astype(jnp.bfloat16)


def draw_queries(key, part):
    fresh = jax.random.normal(jax.random.fold_in(key, 103), (QTOK, QH * HD), jnp.float32)
    fresh = jnp.clip(fresh, -6.0, 6.0) * 3.0
    return fresh.astype(jnp.bfloat16)


def draw_span_starts(key, part):
    first = jax.random.randint(jax.random.fold_in(key, 105), (1,), 0, CACHE - 2 * SPAN_LEN + 1)
    last = jnp.full((1,), CACHE - SPAN_LEN, jnp.int32)
    return jnp.concatenate([first.astype(jnp.int32), last]).astype(jnp.int32)


def set_ends(result, key, low, high):
    spot = [jax.random.randint(jax.random.fold_in(key, axis), (), 0, length) for axis, length in enumerate(result.shape)]
    main_axis = result.shape.index(max(result.shape))
    beside = spot[:main_axis] + [(spot[main_axis] + 1) % result.shape[main_axis]] + spot[main_axis + 1:]
    return result.at[tuple(spot)].set(low).at[tuple(beside)].set(high)


def block_levels(own_key, dims, cuts, least, largest):
    def one(axis_at, blocks):
        steps = jax.random.uniform(jax.random.fold_in(jax.random.fold_in(own_key, 6), axis_at), (blocks,), jnp.float32, least / len(cuts), largest / len(cuts))
        return jnp.repeat(jnp.exp(steps), dims[axis_at] // blocks).reshape((-1,) + (1,) * (len(dims) - axis_at - 1))

    factor_of = one(*cuts[0])
    for cut in cuts[1:]:
        factor_of = factor_of * one(*cut)
    return factor_of


def routed_block(own_key, own, number, rows, amount, top, limit, slope):
    ranking = jax.random.permutation(own_key, amount)
    crowded, ordinary = portions_of(amount, rows * top, limit, slope, True), portions_of(amount, rows * top, limit, slope, False)
    places = jnp.arange(amount)

    def named(sizes, turn):
        used = int((sizes > 0).sum())
        fixed = max(1, used // 4)
        passed = fixed + (places - fixed + turn * (used - fixed)) % max(1, amount - fixed)
        return jnp.zeros((amount,), jnp.int32).at[ranking[jnp.where(places < fixed, places, passed)]].set(jnp.asarray(sizes, jnp.int32))

    sizes = jnp.where(number % 4 == 0, named(crowded, number // 4), named(ordinary, number - number // 4 - 1))
    mixed = jax.random.permutation(jax.random.fold_in(own, 3), amount)
    giver, taker = mixed[0:amount // 2 * 2:2], mixed[1:amount // 2 * 2:2]
    slack = jnp.minimum(sizes[giver] - 1, limit - sizes[taker]) // 2
    slack = jnp.where((giver == ranking[0]) | (taker == ranking[0]) | (sizes[taker] == 0), 0, jnp.maximum(slack, 0))
    passed = jax.random.randint(jax.random.fold_in(own, 4), (amount // 2,), 0, 1 << 20) % (slack + 1)
    sizes = sizes.at[giver].add(-passed).at[taker].add(passed)
    members = jnp.searchsorted(jnp.cumsum(sizes), jnp.arange(rows * top), side="right").astype(jnp.int32)
    table = members.reshape(top, rows).T
    table = table[jax.random.permutation(jax.random.fold_in(own, 1), rows)]
    turn = jax.random.randint(jax.random.fold_in(own, 2), (rows, 1), 0, top)
    return jnp.take_along_axis(table, (jnp.arange(top)[None, :] + turn) % top, axis=1)


def portions_of(count, total, most, slope, full):
    portions = [(1 << 20) // math.isqrt(grade ** slope) + 1 for grade in range(1, count + 1)]
    largest = most if full else min(most, max(-(-total // count), total * portions[0] // sum(portions)))
    least = 1 if total - largest >= count - 1 else 0
    holding, spare = [largest] + [least] * (count - 1), total - largest - least * (count - 1)
    while spare > 0:
        movable = [i for i in range(1, count) if holding[i] < largest] or [i for i in range(1, count) if holding[i] < most]
        whole, left = sum([portions[i] for i in movable]), spare
        for i in movable:
            more = min(most - holding[i], max(1, left * portions[i] // whole), spare)
            holding[i] = holding[i] + more
            spare = spare - more
    return np.array(holding)


def centred(rng, extent, scale, bound, split=(), held_as=jnp.bfloat16):
    level = block_levels(rng, extent, split, -0.22, 0.18) if split else 1.0
    values = jax.random.normal(rng, extent, jnp.float32) * scale * level
    return jnp.minimum(jnp.maximum(values, -bound), bound).astype(held_as)


def setup_inputs(seed: int = 0, part: int = 0) -> dict:
    seeds = jax.random.split(jax.random.key(seed), 12)
    part_splits = jax.random.split(jax.random.fold_in(seeds[11], part), 12)
    queries = draw_queries(jax.random.fold_in(jax.random.fold_in(seeds[11], part), 71), part)
    cache_keys = draw_cache_keys(jax.random.fold_in(jax.random.fold_in(seeds[11], part), 71), part)
    cache_values = centred(part_splits[2], (CACHE, KVH * HD), 1.0, 6.0, ((0, 8), (1, 2)))
    span_starts = draw_span_starts(jax.random.fold_in(jax.random.fold_in(seeds[11], part), 71), part)
    out_weight = centred(seeds[4], (QH * HD, D), (QH * HD) ** -0.5, 0.125, ((0, 16),))
    norm_gain = jnp.clip(1.0 + 0.18 * jax.random.normal(seeds[5], (D,), jnp.float32), 0.099609375, 1.8984375).astype(jnp.bfloat16)
    expert_ids_keys = jax.random.split(jax.random.fold_in(part_splits[6], 1), QTOK // MOE_TOK)
    expert_ids_turns = jax.random.permutation(jax.random.fold_in(part_splits[6], 3), QTOK // MOE_TOK)
    expert_ids = jax.vmap(lambda own, number: routed_block(jax.random.fold_in(part_splits[6], 2), own, number, MOE_TOK, EXPERTS, TOP, CAP, 0))(expert_ids_keys, expert_ids_turns).reshape((QTOK, TOP))
    gate_fixed = set_ends(jax.random.randint(part_splits[7], (QTOK, TOP), 1, 4096), jax.random.fold_in(part_splits[7], 1), 1, 4095).astype(jnp.int32)
    gate_weight = centred(seeds[8], (EXPERTS, D, FF_E), D ** -0.5, 0.125, ((0, 16),))
    up_weight = centred(seeds[9], (EXPERTS, D, FF_E), D ** -0.5, 0.125, ((0, 16),))
    down_weight = centred(seeds[10], (EXPERTS, FF_E, D), FF_E ** -0.5, 0.21875, ((0, 16),))
    return {"queries": queries, "cache_keys": cache_keys, "cache_values": cache_values, "span_starts": span_starts, "out_weight": out_weight, "norm_gain": norm_gain, "expert_ids": expert_ids, "gate_fixed": gate_fixed, "gate_weight": gate_weight, "up_weight": up_weight, "down_weight": down_weight}


NEG_FILL = -1e+30
EPSILON = 1e-06

def reference(queries, cache_keys, cache_values, span_starts, out_weight, norm_gain, expert_ids, gate_fixed, gate_weight, up_weight, down_weight):
    group_size = QH // KVH
    token_index = jnp.arange(QTOK, dtype=jnp.int32)
    query_pos = span_starts[token_index // SPAN_LEN] + token_index % SPAN_LEN
    query_f = queries.astype(jnp.float32).reshape(QTOK, KVH, group_size, HD)
    key_blocks = cache_keys.reshape(N_BLK, CACHE_DEV, KVH, HD)
    value_blocks = cache_values.reshape(N_BLK, CACHE_DEV, KVH, HD)
    score_scale = 1.0 / math.sqrt(HD)

    def one_block(running, item):
        best, numerator, totals = running
        key_block, value_block, block_number = item
        key_pos = block_number * CACHE_DEV + jnp.arange(CACHE_DEV, dtype=jnp.int32)
        visible = (key_pos[None, :] <= query_pos[:, None])[:, None, None, :]
        scores = jnp.einsum('qgjd,kgd->qgjk', query_f, key_block.astype(jnp.float32)) * score_scale
        scores = jnp.where(visible, scores, NEG_FILL)
        block_top = lax.optimization_barrier(jnp.max(scores, axis=-1))
        weights = jnp.where(visible, jnp.exp(scores - block_top[..., None]), 0.0)
        block_sum = lax.optimization_barrier(jnp.sum(weights, axis=-1))
        rounded = weights.astype(jnp.bfloat16).astype(jnp.float32)
        block_out = jnp.einsum('qgjk,kgd->qgjd', rounded, value_block.astype(jnp.float32))
        newest = jnp.maximum(best, block_top)
        old_factor = jnp.exp(best - newest)
        new_factor = jnp.exp(block_top - newest)
        numerator = numerator * old_factor[..., None] + block_out * new_factor[..., None]
        totals = totals * old_factor + block_sum * new_factor
        return ((newest, numerator, totals), None)
    start_best = jnp.full((QTOK, KVH, group_size), NEG_FILL, jnp.float32)
    start_numer = jnp.zeros((QTOK, KVH, group_size, HD), jnp.float32)
    start_totals = jnp.zeros((QTOK, KVH, group_size), jnp.float32)
    block_ids = jnp.arange(N_BLK, dtype=jnp.int32)
    final, unused = lax.scan(one_block, (start_best, start_numer, start_totals), (key_blocks, value_blocks, block_ids))
    attention = (final[1] / final[2][..., None]).reshape(QTOK, QH * HD).astype(jnp.bfloat16)
    attn_proj = jnp.dot(attention, out_weight, preferred_element_type=jnp.float32).astype(jnp.bfloat16)
    values_f = attn_proj.astype(jnp.float32)
    mean_square = lax.optimization_barrier(jnp.mean(values_f * values_f, axis=-1, keepdims=True))
    normed = (values_f * lax.rsqrt(mean_square + EPSILON) * norm_gain.astype(jnp.float32)).astype(jnp.bfloat16)
    gate_values = gate_fixed.astype(jnp.float32)
    route_weight = gate_values / lax.optimization_barrier(jnp.sum(gate_values, axis=1, keepdims=True))

    def one_expert(total, item):
        expert_gate, expert_up, expert_down, expert_number = item
        gate_part = jnp.dot(normed, expert_gate, preferred_element_type=jnp.float32)
        up_part = jnp.dot(normed, expert_up, preferred_element_type=jnp.float32)
        expert_hidden = (jax.nn.silu(gate_part) * up_part).astype(jnp.bfloat16)
        expert_result = jnp.dot(expert_hidden, expert_down, preferred_element_type=jnp.float32).astype(jnp.bfloat16)
        weight_sum = lax.optimization_barrier(jnp.sum(jnp.where(expert_ids == expert_number, route_weight, 0.0), axis=1))
        return (total + weight_sum[:, None] * expert_result.astype(jnp.float32), None)
    expert_numbers = jnp.arange(EXPERTS, dtype=jnp.int32)
    start_total = jnp.zeros((QTOK, D), jnp.float32)
    mixed, unused_two = lax.scan(one_expert, start_total, (gate_weight, up_weight, down_weight, expert_numbers))
    expert_out = mixed.astype(jnp.bfloat16)
    return (attn_proj, expert_out)
```

```python
import functools
import math

import jax
import jax.numpy as jnp
from jax import lax
from jax.experimental import pallas as pl
from jax.experimental.pallas import tpu as pltpu
from jax.sharding import PartitionSpec as P

HD = 128
SPANS = 2


NEG_FILL = -1e30
EPSILON = 1e-06


def partial_attention(query_block, query_pos, cache_keys, cache_values, key_pos):
    rows_here = query_block.shape[0]
    kv_local = cache_keys.shape[1] // HD
    group_size = query_block.shape[1] // (kv_local * HD)
    heads_here = kv_local * group_size
    shaped_q = query_block.reshape(rows_here, kv_local, group_size, HD)
    shaped_k = cache_keys.reshape(-1, kv_local, HD)
    shaped_v = cache_values.reshape(-1, kv_local, HD)
    scores = jnp.einsum(
        "qgjd,kgd->qgjk", shaped_q, shaped_k, preferred_element_type=jnp.float32
    ) * (1.0 / math.sqrt(HD))
    visible = (key_pos[None, :] <= query_pos[:, None])[:, None, None, :]
    scores = jnp.where(visible, scores, NEG_FILL)
    row_top = jnp.max(scores, axis=-1)
    weights = jnp.where(visible, jnp.exp(scores - row_top[..., None]), 0.0)
    totals = jnp.sum(weights, axis=-1)
    numerator = jnp.einsum(
        "qgjk,kgd->qgjd", weights.astype(jnp.bfloat16), shaped_v, preferred_element_type=jnp.float32
    )
    return (
        row_top.reshape(rows_here, heads_here),
        totals.reshape(rows_here, heads_here),
        numerator.reshape(rows_here, heads_here * HD),
    )


def run_experts(arrived, gate_weight, up_weight, down_weight):
    gate_part = jnp.einsum(
        "secd,edf->secf", arrived, gate_weight, preferred_element_type=jnp.float32
    )
    up_part = jnp.einsum("secd,edf->secf", arrived, up_weight, preferred_element_type=jnp.float32)
    hidden = (jax.nn.silu(gate_part) * up_part).astype(jnp.bfloat16)
    return jnp.einsum(
        "secf,efd->secd", hidden, down_weight, preferred_element_type=jnp.float32
    ).astype(jnp.bfloat16)


def on_device(
    queries,
    cache_keys,
    cache_values,
    span_starts,
    out_weight,
    norm_gain,
    expert_ids,
    gate_fixed,
    gate_weight,
    up_weight,
    down_weight,
):
    gathered = lax.all_gather(queries, "blk", axis=0, tiled=True)
    total_rows = gathered.shape[0]
    width = gathered.shape[1]
    span_length = total_rows // SPANS
    token_index = jnp.arange(total_rows, dtype=jnp.int32)
    span_index = token_index // span_length
    span_match = span_index[:, None] == jnp.arange(SPANS, dtype=jnp.int32)[None, :]
    start_of = jnp.sum(jnp.where(span_match, span_starts[None, :], 0), axis=1)
    query_pos = start_of + token_index % span_length
    cache_rows = cache_keys.shape[0]
    key_pos = lax.axis_index("blk") * cache_rows + jnp.arange(cache_rows, dtype=jnp.int32)
    block_rows = math.gcd(total_rows, 128)
    block_count = total_rows // block_rows

    def one_block(item):
        return partial_attention(item[0], item[1], cache_keys, cache_values, key_pos)

    blocked = (
        gathered.reshape(block_count, block_rows, width),
        query_pos.reshape(block_count, block_rows),
    )
    row_top, totals, numerator = lax.map(one_block, blocked)
    heads_here = row_top.shape[2]
    row_top = row_top.reshape(total_rows, heads_here)
    totals = totals.reshape(total_rows, heads_here)
    numerator = numerator.reshape(total_rows, heads_here * HD)
    global_top = lax.pmax(row_top, "blk")
    factor = jnp.exp(row_top - global_top)
    totals = totals * factor
    numerator = (numerator.reshape(total_rows, heads_here, HD) * factor[:, :, None]).reshape(
        total_rows, heads_here * HD
    )
    own_numer = lax.psum_scatter(
        numerator.astype(jnp.bfloat16), "blk", scatter_dimension=1, tiled=True
    ).astype(jnp.float32)
    all_totals = lax.psum(totals, "blk")
    col_width = own_numer.shape[1]
    first_col = lax.axis_index("blk") * col_width
    spread = jnp.repeat(all_totals, HD, axis=1)
    col_totals = lax.dynamic_slice_in_dim(spread, first_col, col_width, 1)
    attended = (own_numer / col_totals).astype(jnp.bfloat16)
    projected = lax.psum_scatter(
        jnp.dot(attended, out_weight, preferred_element_type=jnp.float32),
        ("blk", "rows"),
        scatter_dimension=0,
        tiled=True,
    )
    attn_proj = projected.astype(jnp.bfloat16)
    values_f = attn_proj.astype(jnp.float32)
    mean_square = jnp.mean(values_f * values_f, axis=-1, keepdims=True)
    normed = (values_f * lax.rsqrt(mean_square + EPSILON) * norm_gain.astype(jnp.float32)).astype(
        jnp.bfloat16
    )
    own_tokens = normed.shape[0]
    top_count = expert_ids.shape[1]
    owners = lax.axis_size("blk") * lax.axis_size("rows")
    local_experts = gate_weight.shape[0]
    expert_count = owners * local_experts
    capacity = min(own_tokens, max(2, 2 * top_count * own_tokens // expert_count))
    slot_total = expert_count * capacity
    route_expert = expert_ids.reshape(-1)
    route_count = route_expert.shape[0]
    hits = (route_expert[:, None] == jnp.arange(expert_count, dtype=jnp.int32)[None, :]).astype(
        jnp.int32
    )
    slot_number = jnp.sum(jnp.cumsum(hits, axis=0) * hits, axis=1) - 1
    target = route_expert * capacity + slot_number
    placed = target[:, None] == jnp.arange(slot_total, dtype=jnp.int32)[None, :]
    route_token = jnp.arange(route_count, dtype=jnp.int32) // top_count
    token_pick = route_token[:, None] == jnp.arange(own_tokens, dtype=jnp.int32)[None, :]
    slot_token = jnp.dot(
        placed.astype(jnp.bfloat16).T,
        token_pick.astype(jnp.bfloat16),
        preferred_element_type=jnp.float32,
    ).astype(jnp.bfloat16)
    outgoing = jnp.dot(slot_token, normed, preferred_element_type=jnp.float32).astype(jnp.bfloat16)
    outgoing = outgoing.reshape(owners, local_experts, capacity, -1)
    gate_values = gate_fixed.astype(jnp.float32)
    route_weight = (gate_values / jnp.sum(gate_values, axis=1, keepdims=True)).reshape(-1)
    weighted_pick = token_pick.astype(jnp.float32) * route_weight[:, None]
    blend = jnp.dot(weighted_pick.T, placed.astype(jnp.float32), precision=lax.Precision.HIGHEST)
    finished = run_experts(
        lax.all_to_all(outgoing, ("blk", "rows"), split_axis=0, concat_axis=0, tiled=True),
        gate_weight,
        up_weight,
        down_weight,
    )
    returned = lax.all_to_all(finished, ("blk", "rows"), split_axis=0, concat_axis=0, tiled=True)
    returned_flat = returned.reshape(slot_total, -1)
    mixed = jnp.dot(blend, returned_flat.astype(jnp.float32), precision=lax.Precision.HIGHEST)
    expert_out = mixed.astype(jnp.bfloat16)
    return (attn_proj, expert_out)

def far_of(step, blk):
    return [(at, ((at // 2) ^ step) * 2 + at % 2) for at in range(blk)]


def side_of(size):
    return [(at, at ^ 1) for at in range(size)]


def in_vmem(count):
    return [pl.BlockSpec(memory_space=pltpu.VMEM)] * count


def attend_kernel(sizes, meta, *refs):
    far_count, span_length, cache_rows, heads = sizes
    q_refs = refs[:far_count]
    key_own, key_side, value_own, value_side, ids, gates = refs[far_count : far_count + 6]
    outs = refs[far_count + 6 : 2 * far_count + 6]
    q_all, pos_all, keys, values, staged = refs[2 * far_count + 6 :]
    far, near = meta[0], meta[1]
    piece = q_refs[0].shape[0]
    tokens = far_count * piece
    own_heads = heads // far_count
    for step in range(far_count):
        source = far ^ step
        first = (source * 2 + near) * piece
        base = meta[2 + first // span_length] + first % span_length
        row = pl.multiple_of(source * piece, piece)
        for head in range(heads):
            q_all[pl.ds(head * tokens + row, piece), :] = q_refs[step][:, head * HD : (head + 1) * HD]
        pos_all[pl.ds(row, piece), :] = base + lax.broadcasted_iota(jnp.int32, (piece, HD), 0)
    keys[:cache_rows, :] = key_own[...]
    keys[cache_rows:, :] = key_side[...]
    values[:cache_rows, :] = value_own[...]
    values[cache_rows:, :] = value_side[...]
    lane_at = lax.broadcasted_iota(jnp.int32, (1, 2 * cache_rows), 1)
    own_first = (far * 2 + near) * cache_rows
    side_first = (far * 2 + 1 - near) * cache_rows - cache_rows
    key_pos = lane_at + jnp.where(lane_at < cache_rows, own_first, side_first)
    visible = key_pos <= pos_all[:, :1]
    gate_values = gates[...].astype(jnp.float32)
    route_weight = gate_values / jnp.sum(gate_values, axis=1, keepdims=True)
    own_tokens, top_count = gates.shape
    expert_lane = lax.broadcasted_iota(jnp.int32, (own_tokens, HD), 1) - HD // 2
    weight_of = jnp.zeros((own_tokens, HD), jnp.float32)
    for k in range(top_count):
        weight_of += jnp.where(expert_lane == ids[:, k : k + 1], route_weight[:, k : k + 1], 0.0)
    high = weight_of.astype(jnp.bfloat16).astype(jnp.float32)
    routes = jnp.concatenate(
        [high, weight_of - high, jnp.zeros((tokens - 2 * own_tokens, HD), jnp.float32)], axis=0
    )
    lane = lax.broadcasted_iota(jnp.int32, (tokens, HD), 1)
    scale = 1.0 / math.sqrt(HD)
    for group in range(far_count):
        rows = group * own_heads * tokens
        scores = lax.dot_general(
            q_all[rows : rows + own_heads * tokens, :],
            keys[...],
            (((1,), (1,)), ((), ())),
            preferred_element_type=jnp.float32,
        )
        extra = routes
        weights_16 = []
        for j in range(own_heads):
            part = jnp.where(visible, scores[j * tokens : (j + 1) * tokens] * scale, NEG_FILL)
            top = jnp.maximum(jnp.max(part, axis=1, keepdims=True), NEG_FILL / 10)
            top = top.astype(jnp.bfloat16).astype(jnp.float32)
            weights = jnp.exp(part - top)
            total = jnp.sum(weights, axis=1, keepdims=True)
            total_high = total.astype(jnp.bfloat16).astype(jnp.float32)
            extra = jnp.where(lane == 3 * j, top, extra)
            extra = jnp.where(lane == 3 * j + 1, total_high, extra)
            extra = jnp.where(lane == 3 * j + 2, total - total_high, extra)
            weights_16.append(weights.astype(jnp.bfloat16))
        numerator = jnp.dot(
            jnp.concatenate(weights_16, axis=0), values[...], preferred_element_type=jnp.float32
        ).astype(jnp.bfloat16)
        for j in range(own_heads):
            staged[group, :, j * HD : (j + 1) * HD] = numerator[j * tokens : (j + 1) * tokens]
        staged[group, :, own_heads * HD :] = extra.astype(jnp.bfloat16)
    for step in range(far_count):
        outs[step][...] = staged[far ^ step]


def project_kernel(sizes, meta, *refs):
    far_count, own_heads, own_tokens = sizes
    messages = refs[:far_count]
    weight_own, weight_side, keep, send, routes, partial = refs[far_count:]
    far, near, row_at = meta[0], meta[1], meta[2]
    tokens = messages[0].shape[0]
    attended = []
    extras = [m[:, own_heads * HD :].astype(jnp.float32) for m in messages]
    for j in range(own_heads):
        tops = [e[:, 3 * j : 3 * j + 1] for e in extras]
        best = tops[0]
        for top in tops[1:]:
            best = jnp.maximum(best, top)
        above = jnp.zeros((tokens, HD), jnp.float32)
        below = jnp.zeros((tokens, 1), jnp.float32)
        for top, e, m in zip(tops, extras, messages):
            factor = jnp.exp(top - best)
            above += factor * m[:, j * HD : (j + 1) * HD].astype(jnp.float32)
            below += factor * (e[:, 3 * j + 1 : 3 * j + 2] + e[:, 3 * j + 2 : 3 * j + 3])
        attended.append(above / below)
    first = jnp.where(near == 0, attended[0], attended[1]).astype(jnp.bfloat16)
    second = jnp.where(near == 0, attended[1], attended[0]).astype(jnp.bfloat16)
    partial[...] = jnp.dot(
        first, weight_own[...], preferred_element_type=jnp.float32
    ) + jnp.dot(second, weight_side[...], preferred_element_type=jnp.float32)
    piece = tokens // far_count
    other = 1 - row_at
    mine, theirs = [], []
    for source in range(far_count):
        at = pl.multiple_of(source * piece + row_at * own_tokens, own_tokens)
        mine.append(partial[pl.ds(at, own_tokens), :])
        at = pl.multiple_of(source * piece + other * own_tokens, own_tokens)
        theirs.append(partial[pl.ds(at, own_tokens), :])
    keep[...] = jnp.concatenate(mine, axis=0)
    send[...] = jnp.concatenate(theirs, axis=0).astype(jnp.bfloat16)
    for step in range(far_count):
        e = extras[step]
        at = pl.multiple_of((far ^ step) * own_tokens, own_tokens)
        routes[pl.ds(at, own_tokens), :] = e[:own_tokens] + e[own_tokens : 2 * own_tokens]


def norm_kernel(sizes, meta, *refs):
    far_count, own_tokens = sizes
    parts = refs[:far_count]
    gain, routes, own_rows, spread, summed = refs[far_count:]
    width = gain.shape[1]
    total = parts[0][...].astype(jnp.float32)
    for part in parts[1:]:
        total += part[...].astype(jnp.float32)
    values_f = total.astype(jnp.bfloat16).astype(jnp.float32)
    summed[...] = values_f
    at = pl.multiple_of(meta[0] * own_tokens, own_tokens)
    own_rows[...] = summed[pl.ds(at, own_tokens), :].astype(jnp.bfloat16)
    mean_square = jnp.mean(values_f * values_f, axis=1, keepdims=True)
    spread[:, :width] = (
        values_f * lax.rsqrt(mean_square + EPSILON) * gain[...].astype(jnp.float32)
    ).astype(jnp.bfloat16)
    weight_of = routes[...]
    high = weight_of.astype(jnp.bfloat16).astype(jnp.float32)
    low = pltpu.roll(weight_of - high, HD // 2, 1)
    high = pltpu.roll(high, HD // 2, 1)
    lane = lax.broadcasted_iota(jnp.int32, weight_of.shape, 1)
    spread[:, width:] = jnp.where(
        lane < HD // 2, high, pltpu.roll(low, HD // 2, 1)
    ).astype(jnp.bfloat16)


def expert_kernel(width, meta, *refs):
    pieces = refs[:4]
    gate, up, down, keep, send, gathered, total = refs[4:]
    rows = pieces[0].shape[0]
    step = pl.program_id(0)

    @pl.when(step == 0)
    def _():
        for at, piece in enumerate(pieces):
            gathered[at * rows : (at + 1) * rows, :] = piece[:, :width]
        total[...] = jnp.zeros_like(total)

    arrived = gathered[...]
    gate_part = jnp.dot(arrived, gate[0], preferred_element_type=jnp.float32)
    up_part = jnp.dot(arrived, up[0], preferred_element_type=jnp.float32)
    hidden = (gate_part / (1.0 + jnp.exp(-gate_part)) * up_part).astype(jnp.bfloat16)
    total[...] += jnp.dot(hidden, down[0], preferred_element_type=jnp.float32)

    @pl.when(step == pl.num_programs(0) - 1)
    def _():
        lane = lax.broadcasted_iota(jnp.int32, (rows, HD), 1) % (HD // 2)
        for at, piece in enumerate(pieces):
            routes = piece[:, width:].astype(jnp.float32)
            share = jnp.sum(jnp.where(lane == meta[0], routes, 0.0), axis=1, keepdims=True)
            result = total[at * rows : (at + 1) * rows, :].astype(jnp.bfloat16).astype(jnp.float32)
            target = keep if at < 2 else send
            half = at % 2
            target[half * rows : (half + 1) * rows, :] = (share * result).astype(jnp.bfloat16)


def spread_kernel(sizes, meta, *refs):
    far_count, own_tokens = sizes
    ours, theirs = refs[:2]
    outs = refs[2 : 2 + far_count]
    summed = refs[2 + far_count]
    summed[...] = ours[...].astype(jnp.float32) + theirs[...].astype(jnp.float32)
    for step in range(far_count):
        at = pl.multiple_of((meta[0] ^ step) * own_tokens, own_tokens)
        outs[step][...] = summed[pl.ds(at, own_tokens), :].astype(outs[step].dtype)


def paired_device(
    queries,
    cache_keys,
    cache_values,
    span_starts,
    out_weight,
    norm_gain,
    expert_ids,
    gate_fixed,
    gate_weight,
    up_weight,
    down_weight,
):
    blk, row_count = lax.axis_size("blk"), lax.axis_size("rows")
    far_count = blk // 2
    piece, query_width = queries.shape
    heads = query_width // HD
    own_heads = heads // far_count
    own_tokens = expert_ids.shape[0]
    tokens = far_count * piece
    held = far_count * own_tokens
    width = out_weight.shape[1]
    cache_rows = cache_keys.shape[0]
    span_length = blk * piece // SPANS
    hidden = gate_weight.shape[2]
    blk_at, row_at = lax.axis_index("blk"), lax.axis_index("rows")
    far, near = blk_at // 2, blk_at % 2
    bf16, f32 = jnp.bfloat16, jnp.float32
    smem = pl.BlockSpec(memory_space=pltpu.SMEM)
    shape_of = jax.ShapeDtypeStruct

    def over_far(arrays):
        moved = [lax.ppermute(arrays[step], "blk", far_of(step, blk)) for step in range(far_count - 1, 0, -1)]
        return [arrays[0]] + moved[::-1]

    def over_near(array):
        return lax.ppermute(array, "blk", side_of(blk))

    def over_rows(array):
        return lax.ppermute(array, "rows", side_of(row_count))

    q_pieces = over_far([queries] * far_count)
    key_side, value_side = over_near(cache_keys), over_near(cache_values)
    weight_side = over_near(out_weight)
    place = jnp.concatenate([jnp.stack([far, near]).astype(jnp.int32), span_starts])
    message_width = (own_heads + 1) * HD
    messages = pl.pallas_call(
        functools.partial(attend_kernel, (far_count, span_length, cache_rows, heads)),
        out_shape=[shape_of((tokens, message_width), bf16)] * far_count,
        in_specs=[smem] + in_vmem(far_count + 6),
        out_specs=in_vmem(far_count),
        scratch_shapes=[
            pltpu.VMEM((heads * tokens, HD), bf16),
            pltpu.VMEM((tokens, HD), jnp.int32),
            pltpu.VMEM((2 * cache_rows, HD), bf16),
            pltpu.VMEM((2 * cache_rows, HD), bf16),
            pltpu.VMEM((far_count, tokens, message_width), bf16),
        ],
        name="attend",
    )(place, *q_pieces, cache_keys, key_side, cache_values, value_side, expert_ids, gate_fixed)
    messages = over_far(messages)
    place = jnp.stack([far, near, row_at]).astype(jnp.int32)
    keep, send, routes = pl.pallas_call(
        functools.partial(project_kernel, (far_count, own_heads, own_tokens)),
        out_shape=[shape_of((held, width), f32), shape_of((held, width), bf16), shape_of((held, HD), f32)],
        in_specs=[smem] + in_vmem(far_count + 2),
        out_specs=in_vmem(3),
        scratch_shapes=[pltpu.VMEM((tokens, width), f32)],
        name="project",
    )(place, *messages, out_weight, weight_side)
    part = (keep + over_rows(send).astype(f32)).astype(bf16)
    parts = over_far([part] * far_count)
    place = jnp.stack([far]).astype(jnp.int32)
    attn_proj, normed = pl.pallas_call(
        functools.partial(norm_kernel, (far_count, own_tokens)),
        out_shape=[shape_of((own_tokens, width), bf16), shape_of((held, width + HD), bf16)],
        in_specs=[smem] + in_vmem(far_count + 2),
        out_specs=in_vmem(2),
        scratch_shapes=[pltpu.VMEM((held, width), f32)],
        name="norm",
    )(place, *parts, norm_gain.reshape(1, width), routes)
    from_side = over_near(normed)
    pieces = [normed, from_side, over_rows(normed), over_rows(from_side)]
    chunk = math.gcd(hidden, 256)
    place = jnp.stack([blk_at * row_count + row_at]).astype(jnp.int32)
    whole = pl.BlockSpec((held, width + HD), lambda f: (0, 0))
    keep, send = pl.pallas_call(
        functools.partial(expert_kernel, width),
        out_shape=[shape_of((2 * held, width), bf16)] * 2,
        grid=(hidden // chunk,),
        in_specs=[smem]
        + [whole] * 4
        + [
            pl.BlockSpec((1, width, chunk), lambda f: (0, 0, f)),
            pl.BlockSpec((1, width, chunk), lambda f: (0, 0, f)),
            pl.BlockSpec((1, chunk, width), lambda f: (0, f, 0)),
        ],
        out_specs=[pl.BlockSpec((2 * held, width), lambda f: (0, 0))] * 2,
        scratch_shapes=[pltpu.VMEM((4 * held, width), bf16), pltpu.VMEM((4 * held, width), f32)],
        name="experts",
    )(place, *pieces, gate_weight, up_weight, down_weight)
    both = keep.astype(f32) + over_rows(send).astype(f32)
    ours, theirs = both[:held], both[held:].astype(bf16)
    theirs = over_near(theirs)
    place = jnp.stack([far]).astype(jnp.int32)
    shares = pl.pallas_call(
        functools.partial(spread_kernel, (far_count, own_tokens)),
        out_shape=[shape_of((own_tokens, width), f32)] + [shape_of((own_tokens, width), bf16)] * (far_count - 1),
        in_specs=[smem] + in_vmem(2),
        out_specs=in_vmem(far_count),
        scratch_shapes=[pltpu.VMEM((held, width), f32)],
        name="shares",
    )(place, ours, theirs)
    shares = over_far(shares)
    total = shares[0]
    for share in shares[1:]:
        total = total + share.astype(f32)
    return (attn_proj, total.astype(bf16))


def fits_pairs(mesh, queries, cache_keys, out_weight, expert_ids, gate_weight):
    blk, row_count = mesh.shape["blk"], mesh.shape["rows"]
    parts = mesh.shape["groups"]
    far_count = blk // 2
    if blk % 2 or row_count != 2 or far_count < 2 or far_count & (far_count - 1):
        return False
    heads = queries.shape[1] // (row_count * HD)
    piece = queries.shape[0] // (parts * blk)
    own_tokens = expert_ids.shape[0] // (parts * blk * row_count)
    experts = gate_weight.shape[0]
    return (
        cache_keys.shape[1] == row_count * HD
        and heads == 2 * far_count
        and out_weight.shape[0] == row_count * blk * HD
        and out_weight.shape[1] % HD == 0
        and piece == 2 * own_tokens
        and own_tokens % 8 == 0
        and (blk * piece // SPANS) % piece == 0
        and experts == blk * row_count
        and experts <= HD // 2
        and gate_weight.shape[2] % 128 == 0
    )


def solution(mesh):
    in_specs = (
        P(("groups", "blk"), "rows"),
        P(("groups", "blk"), "rows"),
        P(("groups", "blk"), "rows"),
        P("groups"),
        P(("rows", "blk"), None),
        P(),
        P(("groups", "blk", "rows"), None),
        P(("groups", "blk", "rows"), None),
        P(("blk", "rows"), None, None),
        P(("blk", "rows"), None, None),
        P(("blk", "rows"), None, None),
    )
    out_specs = (P(("groups", "blk", "rows"), None), P(("groups", "blk", "rows"), None))

    def run(*arrays):
        queries, cache_keys, out_weight = arrays[0], arrays[1], arrays[4]
        expert_ids, gate_weight = arrays[6], arrays[8]
        paired = fits_pairs(mesh, queries, cache_keys, out_weight, expert_ids, gate_weight)
        return jax.shard_map(
            paired_device if paired else on_device,
            mesh=mesh,
            in_specs=in_specs,
            out_specs=out_specs,
            check_vma=False,
        )(*arrays)

    return run
```

```python
import functools
import math

import jax
import jax.numpy as jnp
from jax import lax
from jax.experimental import pallas as pl
from jax.experimental.pallas import tpu as pltpu
from jax.sharding import PartitionSpec as P


HD = 128
SPANS = 2


NEG_FILL = -1e30
EPSILON = 1e-06


def partial_attention(query_block, query_pos, cache_keys, cache_values, key_pos):
    rows_here = query_block.shape[0]
    kv_local = cache_keys.shape[1] // HD
    group_size = query_block.shape[1] // (kv_local * HD)
    heads_here = kv_local * group_size
    shaped_q = query_block.reshape(rows_here, kv_local, group_size, HD)
    shaped_k = cache_keys.reshape(-1, kv_local, HD)
    shaped_v = cache_values.reshape(-1, kv_local, HD)
    scores = jnp.einsum(
        "qgjd,kgd->qgjk", shaped_q, shaped_k, preferred_element_type=jnp.float32
    ) * (1.0 / math.sqrt(HD))
    visible = (key_pos[None, :] <= query_pos[:, None])[:, None, None, :]
    scores = jnp.where(visible, scores, NEG_FILL)
    row_top = jnp.max(scores, axis=-1)
    weights = jnp.where(visible, jnp.exp(scores - row_top[..., None]), 0.0)
    totals = jnp.sum(weights, axis=-1)
    numerator = jnp.einsum(
        "qgjk,kgd->qgjd", weights.astype(jnp.bfloat16), shaped_v, preferred_element_type=jnp.float32
    )
    return (
        row_top.reshape(rows_here, heads_here),
        totals.reshape(rows_here, heads_here),
        numerator.reshape(rows_here, heads_here * HD),
    )


def run_experts(arrived, gate_weight, up_weight, down_weight):
    gate_part = jnp.einsum(
        "secd,edf->secf", arrived, gate_weight, preferred_element_type=jnp.float32
    )
    up_part = jnp.einsum("secd,edf->secf", arrived, up_weight, preferred_element_type=jnp.float32)
    hidden = (jax.nn.silu(gate_part) * up_part).astype(jnp.bfloat16)
    return jnp.einsum(
        "secf,efd->secd", hidden, down_weight, preferred_element_type=jnp.float32
    ).astype(jnp.bfloat16)


def on_device(
    queries,
    cache_keys,
    cache_values,
    span_starts,
    out_weight,
    norm_gain,
    expert_ids,
    gate_fixed,
    gate_weight,
    up_weight,
    down_weight,
):
    gathered = lax.all_gather(queries, "blk", axis=0, tiled=True)
    total_rows = gathered.shape[0]
    width = gathered.shape[1]
    span_length = total_rows // SPANS
    token_index = jnp.arange(total_rows, dtype=jnp.int32)
    span_index = token_index // span_length
    span_match = span_index[:, None] == jnp.arange(SPANS, dtype=jnp.int32)[None, :]
    start_of = jnp.sum(jnp.where(span_match, span_starts[None, :], 0), axis=1)
    query_pos = start_of + token_index % span_length
    cache_rows = cache_keys.shape[0]
    key_pos = lax.axis_index("blk") * cache_rows + jnp.arange(cache_rows, dtype=jnp.int32)
    block_rows = math.gcd(total_rows, 128)
    block_count = total_rows // block_rows

    def one_block(item):
        return partial_attention(item[0], item[1], cache_keys, cache_values, key_pos)

    blocked = (
        gathered.reshape(block_count, block_rows, width),
        query_pos.reshape(block_count, block_rows),
    )
    row_top, totals, numerator = lax.map(one_block, blocked)
    heads_here = row_top.shape[2]
    row_top = row_top.reshape(total_rows, heads_here)
    totals = totals.reshape(total_rows, heads_here)
    numerator = numerator.reshape(total_rows, heads_here * HD)
    global_top = lax.pmax(row_top, "blk")
    factor = jnp.exp(row_top - global_top)
    totals = totals * factor
    numerator = (numerator.reshape(total_rows, heads_here, HD) * factor[:, :, None]).reshape(
        total_rows, heads_here * HD
    )
    own_numer = lax.psum_scatter(
        numerator.astype(jnp.bfloat16), "blk", scatter_dimension=1, tiled=True
    ).astype(jnp.float32)
    all_totals = lax.psum(totals, "blk")
    col_width = own_numer.shape[1]
    first_col = lax.axis_index("blk") * col_width
    spread = jnp.repeat(all_totals, HD, axis=1)
    col_totals = lax.dynamic_slice_in_dim(spread, first_col, col_width, 1)
    attended = (own_numer / col_totals).astype(jnp.bfloat16)
    projected = lax.psum_scatter(
        jnp.dot(attended, out_weight, preferred_element_type=jnp.float32),
        ("blk", "rows"),
        scatter_dimension=0,
        tiled=True,
    )
    attn_proj = projected.astype(jnp.bfloat16)
    values_f = attn_proj.astype(jnp.float32)
    mean_square = jnp.mean(values_f * values_f, axis=-1, keepdims=True)
    normed = (values_f * lax.rsqrt(mean_square + EPSILON) * norm_gain.astype(jnp.float32)).astype(
        jnp.bfloat16
    )
    own_tokens = normed.shape[0]
    top_count = expert_ids.shape[1]
    owners = lax.axis_size("blk") * lax.axis_size("rows")
    local_experts = gate_weight.shape[0]
    expert_count = owners * local_experts
    capacity = min(own_tokens, max(2, 2 * top_count * own_tokens // expert_count))
    slot_total = expert_count * capacity
    route_expert = expert_ids.reshape(-1)
    route_count = route_expert.shape[0]
    hits = (route_expert[:, None] == jnp.arange(expert_count, dtype=jnp.int32)[None, :]).astype(
        jnp.int32
    )
    slot_number = jnp.sum(jnp.cumsum(hits, axis=0) * hits, axis=1) - 1
    target = route_expert * capacity + slot_number
    placed = target[:, None] == jnp.arange(slot_total, dtype=jnp.int32)[None, :]
    route_token = jnp.arange(route_count, dtype=jnp.int32) // top_count
    token_pick = route_token[:, None] == jnp.arange(own_tokens, dtype=jnp.int32)[None, :]
    slot_token = jnp.dot(
        placed.astype(jnp.bfloat16).T,
        token_pick.astype(jnp.bfloat16),
        preferred_element_type=jnp.float32,
    ).astype(jnp.bfloat16)
    outgoing = jnp.dot(slot_token, normed, preferred_element_type=jnp.float32).astype(jnp.bfloat16)
    outgoing = outgoing.reshape(owners, local_experts, capacity, -1)
    gate_values = gate_fixed.astype(jnp.float32)
    route_weight = (gate_values / jnp.sum(gate_values, axis=1, keepdims=True)).reshape(-1)
    weighted_pick = token_pick.astype(jnp.float32) * route_weight[:, None]
    blend = jnp.dot(weighted_pick.T, placed.astype(jnp.float32), precision=lax.Precision.HIGHEST)
    finished = run_experts(
        lax.all_to_all(outgoing, ("blk", "rows"), split_axis=0, concat_axis=0, tiled=True),
        gate_weight,
        up_weight,
        down_weight,
    )
    returned = lax.all_to_all(finished, ("blk", "rows"), split_axis=0, concat_axis=0, tiled=True)
    returned_flat = returned.reshape(slot_total, -1)
    mixed = jnp.dot(blend, returned_flat.astype(jnp.float32), precision=lax.Precision.HIGHEST)
    expert_out = mixed.astype(jnp.bfloat16)
    return (attn_proj, expert_out)


def far_of(step, blk):
    return [(at, ((at // 2) ^ step) * 2 + at % 2) for at in range(blk)]


def side_of(size):
    return [(at, at ^ 1) for at in range(size)]


def place_of():
    blk_at = lax.axis_index("blk")
    return blk_at // 2, blk_at % 2


def grant(mebibytes):
    return pltpu.CompilerParams(vmem_limit_bytes=mebibytes << 20)


def in_vmem(count):
    return [pl.BlockSpec(memory_space=pltpu.VMEM)] * count


def prepare_kernel(sizes, *refs):
    far_count, span_length = sizes
    sources, (starts_hbm, ids_hbm, gates_hbm) = refs[:7], refs[7:10]
    targets, (pos_all, routes) = refs[10:17], refs[17:19]
    starts, ids_ref, gates_ref, sems = refs[19:]
    copies = [
        pltpu.make_async_copy(source, target, sems.at[at])
        for at, (source, target) in enumerate(
            zip((starts_hbm, ids_hbm, gates_hbm) + sources, (starts, ids_ref, gates_ref) + targets)
        )
    ]
    for copy in copies:
        copy.start()
    for copy in copies[:3]:
        copy.wait()
    _, near = place_of()
    tokens = pos_all.shape[0]
    piece = tokens // far_count
    for source in range(far_count):
        first = (source * 2 + near) * piece
        base = starts[first // span_length] + first % span_length
        pos_all[source * piece : (source + 1) * piece, :] = base + lax.broadcasted_iota(
            jnp.int32, (piece, HD), 0
        )
    gate_values = gates_ref[...].astype(jnp.float32)
    ids = ids_ref[...]
    route_weight = gate_values / jnp.sum(gate_values, axis=1, keepdims=True)
    own_tokens, top_count = gate_values.shape
    expert_lane = lax.broadcasted_iota(jnp.int32, (own_tokens, HD), 1) - HD // 2
    weight_of = jnp.zeros((own_tokens, HD), jnp.float32)
    for k in range(top_count):
        weight_of += jnp.where(expert_lane == ids[:, k : k + 1], route_weight[:, k : k + 1], 0.0)
    high = weight_of.astype(jnp.bfloat16).astype(jnp.float32)
    routes[...] = jnp.concatenate(
        [high, weight_of - high, jnp.zeros((tokens - 2 * own_tokens, HD), jnp.float32)], axis=0
    )
    for copy in copies[3:]:
        copy.wait()


def attend_kernel(sizes, *refs):
    far_count, cache_rows, heads = sizes
    q_refs = refs[:far_count]
    key_own, key_side, value_own, value_side, pos_all, routes_ref = refs[far_count : far_count + 6]
    outs = refs[far_count + 6 : 2 * far_count + 6]
    q_all, keys, values, staged = refs[2 * far_count + 6 :]
    far, near = place_of()
    piece = q_refs[0].shape[0]
    tokens = far_count * piece
    own_heads = heads // far_count
    for step in range(far_count):
        source = far ^ step
        row = pl.multiple_of(source * piece, piece)
        for head in range(heads):
            q_all[pl.ds(head * tokens + row, piece), :] = q_refs[step][:, head * HD : (head + 1) * HD]
    keys[:cache_rows, :] = key_own[...]
    keys[cache_rows:, :] = key_side[...]
    values[:cache_rows, :] = value_own[...]
    values[cache_rows:, :] = value_side[...]
    lane_at = lax.broadcasted_iota(jnp.int32, (1, 2 * cache_rows), 1)
    own_first = (far * 2 + near) * cache_rows
    side_first = (far * 2 + 1 - near) * cache_rows - cache_rows
    key_pos = lane_at + jnp.where(lane_at < cache_rows, own_first, side_first)
    visible = key_pos <= pos_all[:, :1]
    routes = routes_ref[...]
    lane = lax.broadcasted_iota(jnp.int32, (tokens, HD), 1)
    scale = 1.0 / math.sqrt(HD)
    for group in range(far_count):
        rows = group * own_heads * tokens
        scores = lax.dot_general(
            q_all[rows : rows + own_heads * tokens, :],
            keys[...],
            (((1,), (1,)), ((), ())),
            preferred_element_type=jnp.float32,
        )
        extra = routes
        weights_16 = []
        for j in range(own_heads):
            part = jnp.where(visible, scores[j * tokens : (j + 1) * tokens] * scale, NEG_FILL)
            top = jnp.maximum(jnp.max(part, axis=1, keepdims=True), NEG_FILL / 10)
            top = top.astype(jnp.bfloat16).astype(jnp.float32)
            weights = jnp.exp(part - top)
            total = jnp.sum(weights, axis=1, keepdims=True)
            total_high = total.astype(jnp.bfloat16).astype(jnp.float32)
            extra = jnp.where(lane == 3 * j, top, extra)
            extra = jnp.where(lane == 3 * j + 1, total_high, extra)
            extra = jnp.where(lane == 3 * j + 2, total - total_high, extra)
            weights_16.append(weights.astype(jnp.bfloat16))
        numerator = jnp.dot(
            jnp.concatenate(weights_16, axis=0), values[...], preferred_element_type=jnp.float32
        ).astype(jnp.bfloat16)
        for j in range(own_heads):
            staged[group, :, j * HD : (j + 1) * HD] = numerator[j * tokens : (j + 1) * tokens]
        staged[group, :, own_heads * HD :] = extra.astype(jnp.bfloat16)
    for step in range(far_count):
        outs[step][...] = staged[far ^ step]


def project_kernel(sizes, *refs):
    far_count, own_heads, own_tokens = sizes
    messages = refs[:far_count]
    weight_own, weight_side, keep, send, routes, partial = refs[far_count:]
    far, near = place_of()
    row_at = lax.axis_index("rows")
    tokens = messages[0].shape[0]
    attended = []
    extras = [m[:, own_heads * HD :].astype(jnp.float32) for m in messages]
    for j in range(own_heads):
        tops = [e[:, 3 * j : 3 * j + 1] for e in extras]
        best = tops[0]
        for top in tops[1:]:
            best = jnp.maximum(best, top)
        above = jnp.zeros((tokens, HD), jnp.float32)
        below = jnp.zeros((tokens, 1), jnp.float32)
        for top, e, m in zip(tops, extras, messages):
            factor = jnp.exp(top - best)
            above += factor * m[:, j * HD : (j + 1) * HD].astype(jnp.float32)
            below += factor * (e[:, 3 * j + 1 : 3 * j + 2] + e[:, 3 * j + 2 : 3 * j + 3])
        attended.append(above / below)
    first = jnp.where(near == 0, attended[0], attended[1]).astype(jnp.bfloat16)
    second = jnp.where(near == 0, attended[1], attended[0]).astype(jnp.bfloat16)
    partial[...] = jnp.dot(
        first, weight_own[...], preferred_element_type=jnp.float32
    ) + jnp.dot(second, weight_side[...], preferred_element_type=jnp.float32)
    piece = tokens // far_count
    other = 1 - row_at
    mine, theirs = [], []
    for source in range(far_count):
        at = pl.multiple_of(source * piece + row_at * own_tokens, own_tokens)
        mine.append(partial[pl.ds(at, own_tokens), :])
        at = pl.multiple_of(source * piece + other * own_tokens, own_tokens)
        theirs.append(partial[pl.ds(at, own_tokens), :])
    keep[...] = jnp.concatenate(mine, axis=0)
    send[...] = jnp.concatenate(theirs, axis=0).astype(jnp.bfloat16)
    for step in range(far_count):
        e = extras[step]
        at = pl.multiple_of((far ^ step) * own_tokens, own_tokens)
        routes[pl.ds(at, own_tokens), :] = e[:own_tokens] + e[own_tokens : 2 * own_tokens]


def norm_kernel(sizes, *refs):
    far_count, own_tokens = sizes
    parts = refs[:far_count]
    gain, routes, own_rows, spread, summed = refs[far_count:]
    width = gain.shape[1]
    total = parts[0][...].astype(jnp.float32)
    for part in parts[1:]:
        total += part[...].astype(jnp.float32)
    values_f = total.astype(jnp.bfloat16).astype(jnp.float32)
    summed[...] = values_f
    at = pl.multiple_of(place_of()[0] * own_tokens, own_tokens)
    own_rows[...] = summed[pl.ds(at, own_tokens), :].astype(jnp.bfloat16)
    mean_square = jnp.mean(values_f * values_f, axis=1, keepdims=True)
    spread[:, :width] = (
        values_f * lax.rsqrt(mean_square + EPSILON) * gain[...].astype(jnp.float32)
    ).astype(jnp.bfloat16)
    weight_of = routes[...]
    high = weight_of.astype(jnp.bfloat16).astype(jnp.float32)
    low = pltpu.roll(weight_of - high, HD // 2, 1)
    high = pltpu.roll(high, HD // 2, 1)
    lane = lax.broadcasted_iota(jnp.int32, weight_of.shape, 1)
    spread[:, width:] = jnp.where(
        lane < HD // 2, high, pltpu.roll(low, HD // 2, 1)
    ).astype(jnp.bfloat16)


def expert_kernel(width, *refs):
    pieces = refs[:4]
    gate, up, down, keep, send, gathered, hidden = refs[4:]
    rows = pieces[0].shape[0]
    for at, piece in enumerate(pieces):
        gathered[at * rows : (at + 1) * rows, :] = piece[:, :width]
    arrived = gathered[...]
    ff = hidden.shape[1]
    chunk = math.gcd(ff, 256)
    for first in range(0, ff, chunk):
        gate_part = jnp.dot(
            arrived, gate[0, :, first : first + chunk], preferred_element_type=jnp.float32
        )
        up_part = jnp.dot(
            arrived, up[0, :, first : first + chunk], preferred_element_type=jnp.float32
        )
        hidden[:, first : first + chunk] = (
            gate_part / (1.0 + jnp.exp(-gate_part)) * up_part
        ).astype(jnp.bfloat16)
    expert = lax.axis_index("blk") * 2 + lax.axis_index("rows")
    lane = lax.broadcasted_iota(jnp.int32, (rows, HD), 1) % (HD // 2)
    shares = []
    for piece in pieces:
        routes = piece[:, width:].astype(jnp.float32)
        shares.append(jnp.sum(jnp.where(lane == expert, routes, 0.0), axis=1, keepdims=True))
    acted = hidden[...]
    for first in range(0, width, 512):
        last = min(first + 512, width)
        result = jnp.dot(acted, down[0, :, first:last], preferred_element_type=jnp.float32)
        result = result.astype(jnp.bfloat16).astype(jnp.float32)
        for at, share in enumerate(shares):
            target = keep if at < 2 else send
            half = at % 2
            target[half * rows : (half + 1) * rows, first:last] = (
                share * result[at * rows : (at + 1) * rows]
            ).astype(jnp.bfloat16)


def add_kernel(*refs):
    terms, out = refs[:-1], refs[-1]
    total = terms[0][...].astype(jnp.float32)
    for term in terms[1:]:
        total += term[...].astype(jnp.float32)
    out[...] = total.astype(out.dtype)


def halves_kernel(keep, received, ours, theirs):
    held = ours.shape[0]
    ours[...] = keep[:held, :].astype(jnp.float32) + received[:held, :].astype(jnp.float32)
    theirs[...] = (
        keep[held:, :].astype(jnp.float32) + received[held:, :].astype(jnp.float32)
    ).astype(jnp.bfloat16)


def spread_kernel(sizes, *refs):
    far_count, own_tokens = sizes
    ours, theirs = refs[:2]
    outs = refs[2 : 2 + far_count]
    summed = refs[2 + far_count]
    summed[...] = ours[...].astype(jnp.float32) + theirs[...].astype(jnp.float32)
    for step in range(far_count):
        at = pl.multiple_of((place_of()[0] ^ step) * own_tokens, own_tokens)
        outs[step][...] = summed[pl.ds(at, own_tokens), :].astype(outs[step].dtype)


def paired_device(
    queries,
    cache_keys,
    cache_values,
    span_starts,
    out_weight,
    norm_gain,
    expert_ids,
    gate_fixed,
    gate_weight,
    up_weight,
    down_weight,
):
    blk, row_count = lax.axis_size("blk"), lax.axis_size("rows")
    far_count = blk // 2
    piece, query_width = queries.shape
    heads = query_width // HD
    own_heads = heads // far_count
    own_tokens = expert_ids.shape[0]
    tokens = far_count * piece
    held = far_count * own_tokens
    width = out_weight.shape[1]
    cache_rows = cache_keys.shape[0]
    span_length = blk * piece // SPANS
    hidden = gate_weight.shape[2]
    bf16, f32 = jnp.bfloat16, jnp.float32
    shape_of = jax.ShapeDtypeStruct

    def over_far(arrays):
        moved = []
        for step in range(far_count - 1, 0, -1):
            moved.append(lax.ppermute(arrays[step], "blk", far_of(step, blk)))
        return [arrays[0]] + moved[::-1]

    def added(shape, dtype, *terms):
        return pl.pallas_call(
            add_kernel,
            out_shape=shape_of(shape, dtype),
            in_specs=in_vmem(len(terms)),
            out_specs=pl.BlockSpec(memory_space=pltpu.VMEM),
            compiler_params=grant(4),
            name="added",
        )(*terms)

    def over_near(array):
        return lax.ppermute(array, "blk", side_of(blk))

    def over_rows(array):
        return lax.ppermute(array, "rows", side_of(row_count))

    key_side = over_near(cache_keys)
    value_side = over_near(cache_values)
    q_pieces = over_far([queries] * far_count)
    weight_side = over_near(out_weight)
    local = [queries, cache_keys, cache_values, out_weight, gate_weight, up_weight, down_weight]
    *local, pos_all, routes = pl.pallas_call(
        functools.partial(prepare_kernel, (far_count, span_length)),
        out_shape=[shape_of(a.shape, a.dtype) for a in local]
        + [shape_of((tokens, HD), jnp.int32), shape_of((tokens, HD), f32)],
        in_specs=[pl.BlockSpec(memory_space=pltpu.HBM)] * 10,
        out_specs=in_vmem(9),
        scratch_shapes=[
            pltpu.SMEM(span_starts.shape, jnp.int32),
            pltpu.VMEM(expert_ids.shape, jnp.int32),
            pltpu.VMEM(gate_fixed.shape, jnp.int32),
            pltpu.SemaphoreType.DMA((10,)),
        ],
        compiler_params=grant(4),
        name="prepare",
    )(*(pltpu.with_memory_space_constraint(a, pltpu.HBM) for a in local + [span_starts, expert_ids, gate_fixed]))
    queries_own, keys_own, values_own, weight_own, gate_weight, up_weight, down_weight = local
    q_pieces[0] = queries_own
    message_width = (own_heads + 1) * HD
    messages = pl.pallas_call(
        functools.partial(attend_kernel, (far_count, cache_rows, heads)),
        out_shape=[shape_of((tokens, message_width), bf16)] * far_count,
        in_specs=in_vmem(far_count + 6),
        out_specs=in_vmem(far_count),
        scratch_shapes=[
            pltpu.VMEM((heads * tokens, HD), bf16),
            pltpu.VMEM((2 * cache_rows, HD), bf16),
            pltpu.VMEM((2 * cache_rows, HD), bf16),
            pltpu.VMEM((far_count, tokens, message_width), bf16),
        ],
        compiler_params=grant(12),
        name="attend",
    )(*q_pieces, keys_own, key_side, values_own, value_side, pos_all, routes)
    messages = over_far(messages)
    keep, send, routes = pl.pallas_call(
        functools.partial(project_kernel, (far_count, own_heads, own_tokens)),
        out_shape=[shape_of((held, width), f32), shape_of((held, width), bf16), shape_of((held, HD), f32)],
        in_specs=in_vmem(far_count + 2),
        out_specs=in_vmem(3),
        scratch_shapes=[pltpu.VMEM((tokens, width), f32)],
        compiler_params=grant(8),
        name="project",
    )(*messages, weight_own, weight_side)
    part = added((held, width), bf16, keep, over_rows(send))
    parts = over_far([part] * far_count)
    attn_proj, normed = pl.pallas_call(
        functools.partial(norm_kernel, (far_count, own_tokens)),
        out_shape=[shape_of((own_tokens, width), bf16), shape_of((held, width + HD), bf16)],
        in_specs=in_vmem(far_count + 2),
        out_specs=in_vmem(2),
        scratch_shapes=[pltpu.VMEM((held, width), f32)],
        compiler_params=grant(6),
        name="norm",
    )(*parts, norm_gain.reshape(1, width), routes)
    from_side = over_near(normed)
    pieces = [normed, from_side, over_rows(normed), over_rows(from_side)]
    keep, send = pl.pallas_call(
        functools.partial(expert_kernel, width),
        out_shape=[shape_of((2 * held, width), bf16)] * 2,
        in_specs=in_vmem(7),
        out_specs=in_vmem(2),
        scratch_shapes=[pltpu.VMEM((4 * held, width), bf16), pltpu.VMEM((4 * held, hidden), bf16)],
        compiler_params=grant(8),
        name="experts",
    )(*pieces, gate_weight, up_weight, down_weight)
    ours, theirs = pl.pallas_call(
        halves_kernel,
        out_shape=[shape_of((held, width), f32), shape_of((held, width), bf16)],
        in_specs=in_vmem(2),
        out_specs=in_vmem(2),
        compiler_params=grant(4),
        name="halves",
    )(keep, over_rows(send))
    theirs = over_near(theirs)
    shares = pl.pallas_call(
        functools.partial(spread_kernel, (far_count, own_tokens)),
        out_shape=[shape_of((own_tokens, width), f32)] + [shape_of((own_tokens, width), bf16)] * (far_count - 1),
        in_specs=in_vmem(2),
        out_specs=in_vmem(far_count),
        scratch_shapes=[pltpu.VMEM((held, width), f32)],
        compiler_params=grant(4),
        name="shares",
    )(ours, theirs)
    shares = over_far(shares)
    return (attn_proj, added((own_tokens, width), bf16, *shares))


def fits_pairs(mesh, queries, cache_keys, out_weight, expert_ids, gate_weight):
    blk, row_count = mesh.shape["blk"], mesh.shape["rows"]
    parts = mesh.shape["groups"]
    far_count = blk // 2
    if blk % 2 or row_count != 2 or far_count < 2 or far_count & (far_count - 1):
        return False
    heads = queries.shape[1] // (row_count * HD)
    piece = queries.shape[0] // (parts * blk)
    own_tokens = expert_ids.shape[0] // (parts * blk * row_count)
    experts = gate_weight.shape[0]
    return (
        cache_keys.shape[1] == row_count * HD
        and heads == 2 * far_count
        and out_weight.shape[0] == row_count * blk * HD
        and out_weight.shape[1] % HD == 0
        and piece == 2 * own_tokens
        and own_tokens % 8 == 0
        and (blk * piece // SPANS) % piece == 0
        and experts == blk * row_count
        and experts <= HD // 2
        and gate_weight.shape[2] % 128 == 0
    )


def solution(mesh):
    in_specs = (
        P(("groups", "blk"), "rows"),
        P(("groups", "blk"), "rows"),
        P(("groups", "blk"), "rows"),
        P("groups"),
        P(("rows", "blk"), None),
        P(),
        P(("groups", "blk", "rows"), None),
        P(("groups", "blk", "rows"), None),
        P(("blk", "rows"), None, None),
        P(("blk", "rows"), None, None),
        P(("blk", "rows"), None, None),
    )
    out_specs = (P(("groups", "blk", "rows"), None), P(("groups", "blk", "rows"), None))

    def mapped(body):
        return jax.shard_map(
            body, mesh=mesh, in_specs=in_specs, out_specs=out_specs, check_vma=False
        )

    def run(*arrays):
        queries, cache_keys, out_weight = arrays[0], arrays[1], arrays[4]
        expert_ids, gate_weight = arrays[6], arrays[8]
        if not fits_pairs(mesh, queries, cache_keys, out_weight, expert_ids, gate_weight):
            return mapped(on_device)(*arrays)
        return mapped(paired_device)(*arrays)

    return run
```

```python
import functools
import math

import jax
import jax.numpy as jnp
from jax import lax
from jax.experimental import pallas as pl
from jax.experimental.pallas import tpu as pltpu
from jax.sharding import PartitionSpec as P


HD = 128
SPANS = 2


NEG_FILL = -1e30
EPSILON = 1e-06


def partial_attention(query_block, query_pos, cache_keys, cache_values, key_pos):
    rows_here = query_block.shape[0]
    kv_local = cache_keys.shape[1] // HD
    group_size = query_block.shape[1] // (kv_local * HD)
    heads_here = kv_local * group_size
    shaped_q = query_block.reshape(rows_here, kv_local, group_size, HD)
    shaped_k = cache_keys.reshape(-1, kv_local, HD)
    shaped_v = cache_values.reshape(-1, kv_local, HD)
    scores = jnp.einsum(
        "qgjd,kgd->qgjk", shaped_q, shaped_k, preferred_element_type=jnp.float32
    ) * (1.0 / math.sqrt(HD))
    visible = (key_pos[None, :] <= query_pos[:, None])[:, None, None, :]
    scores = jnp.where(visible, scores, NEG_FILL)
    row_top = jnp.max(scores, axis=-1)
    weights = jnp.where(visible, jnp.exp(scores - row_top[..., None]), 0.0)
    totals = jnp.sum(weights, axis=-1)
    numerator = jnp.einsum(
        "qgjk,kgd->qgjd", weights.astype(jnp.bfloat16), shaped_v, preferred_element_type=jnp.float32
    )
    return (
        row_top.reshape(rows_here, heads_here),
        totals.reshape(rows_here, heads_here),
        numerator.reshape(rows_here, heads_here * HD),
    )


def run_experts(arrived, gate_weight, up_weight, down_weight):
    gate_part = jnp.einsum(
        "secd,edf->secf", arrived, gate_weight, preferred_element_type=jnp.float32
    )
    up_part = jnp.einsum("secd,edf->secf", arrived, up_weight, preferred_element_type=jnp.float32)
    hidden = (jax.nn.silu(gate_part) * up_part).astype(jnp.bfloat16)
    return jnp.einsum(
        "secf,efd->secd", hidden, down_weight, preferred_element_type=jnp.float32
    ).astype(jnp.bfloat16)


def on_device(
    queries,
    cache_keys,
    cache_values,
    span_starts,
    out_weight,
    norm_gain,
    expert_ids,
    gate_fixed,
    gate_weight,
    up_weight,
    down_weight,
):
    gathered = lax.all_gather(queries, "blk", axis=0, tiled=True)
    total_rows = gathered.shape[0]
    width = gathered.shape[1]
    span_length = total_rows // SPANS
    token_index = jnp.arange(total_rows, dtype=jnp.int32)
    span_index = token_index // span_length
    span_match = span_index[:, None] == jnp.arange(SPANS, dtype=jnp.int32)[None, :]
    start_of = jnp.sum(jnp.where(span_match, span_starts[None, :], 0), axis=1)
    query_pos = start_of + token_index % span_length
    cache_rows = cache_keys.shape[0]
    key_pos = lax.axis_index("blk") * cache_rows + jnp.arange(cache_rows, dtype=jnp.int32)
    block_rows = math.gcd(total_rows, 128)
    block_count = total_rows // block_rows

    def one_block(item):
        return partial_attention(item[0], item[1], cache_keys, cache_values, key_pos)

    blocked = (
        gathered.reshape(block_count, block_rows, width),
        query_pos.reshape(block_count, block_rows),
    )
    row_top, totals, numerator = lax.map(one_block, blocked)
    heads_here = row_top.shape[2]
    row_top = row_top.reshape(total_rows, heads_here)
    totals = totals.reshape(total_rows, heads_here)
    numerator = numerator.reshape(total_rows, heads_here * HD)
    global_top = lax.pmax(row_top, "blk")
    factor = jnp.exp(row_top - global_top)
    totals = totals * factor
    numerator = (numerator.reshape(total_rows, heads_here, HD) * factor[:, :, None]).reshape(
        total_rows, heads_here * HD
    )
    own_numer = lax.psum_scatter(
        numerator.astype(jnp.bfloat16), "blk", scatter_dimension=1, tiled=True
    ).astype(jnp.float32)
    all_totals = lax.psum(totals, "blk")
    col_width = own_numer.shape[1]
    first_col = lax.axis_index("blk") * col_width
    spread = jnp.repeat(all_totals, HD, axis=1)
    col_totals = lax.dynamic_slice_in_dim(spread, first_col, col_width, 1)
    attended = (own_numer / col_totals).astype(jnp.bfloat16)
    projected = lax.psum_scatter(
        jnp.dot(attended, out_weight, preferred_element_type=jnp.float32),
        ("blk", "rows"),
        scatter_dimension=0,
        tiled=True,
    )
    attn_proj = projected.astype(jnp.bfloat16)
    values_f = attn_proj.astype(jnp.float32)
    mean_square = jnp.mean(values_f * values_f, axis=-1, keepdims=True)
    normed = (values_f * lax.rsqrt(mean_square + EPSILON) * norm_gain.astype(jnp.float32)).astype(
        jnp.bfloat16
    )
    own_tokens = normed.shape[0]
    top_count = expert_ids.shape[1]
    owners = lax.axis_size("blk") * lax.axis_size("rows")
    local_experts = gate_weight.shape[0]
    expert_count = owners * local_experts
    capacity = min(own_tokens, max(2, 2 * top_count * own_tokens // expert_count))
    slot_total = expert_count * capacity
    route_expert = expert_ids.reshape(-1)
    route_count = route_expert.shape[0]
    hits = (route_expert[:, None] == jnp.arange(expert_count, dtype=jnp.int32)[None, :]).astype(
        jnp.int32
    )
    slot_number = jnp.sum(jnp.cumsum(hits, axis=0) * hits, axis=1) - 1
    target = route_expert * capacity + slot_number
    placed = target[:, None] == jnp.arange(slot_total, dtype=jnp.int32)[None, :]
    route_token = jnp.arange(route_count, dtype=jnp.int32) // top_count
    token_pick = route_token[:, None] == jnp.arange(own_tokens, dtype=jnp.int32)[None, :]
    slot_token = jnp.dot(
        placed.astype(jnp.bfloat16).T,
        token_pick.astype(jnp.bfloat16),
        preferred_element_type=jnp.float32,
    ).astype(jnp.bfloat16)
    outgoing = jnp.dot(slot_token, normed, preferred_element_type=jnp.float32).astype(jnp.bfloat16)
    outgoing = outgoing.reshape(owners, local_experts, capacity, -1)
    gate_values = gate_fixed.astype(jnp.float32)
    route_weight = (gate_values / jnp.sum(gate_values, axis=1, keepdims=True)).reshape(-1)
    weighted_pick = token_pick.astype(jnp.float32) * route_weight[:, None]
    blend = jnp.dot(weighted_pick.T, placed.astype(jnp.float32), precision=lax.Precision.HIGHEST)
    finished = run_experts(
        lax.all_to_all(outgoing, ("blk", "rows"), split_axis=0, concat_axis=0, tiled=True),
        gate_weight,
        up_weight,
        down_weight,
    )
    returned = lax.all_to_all(finished, ("blk", "rows"), split_axis=0, concat_axis=0, tiled=True)
    returned_flat = returned.reshape(slot_total, -1)
    mixed = jnp.dot(blend, returned_flat.astype(jnp.float32), precision=lax.Precision.HIGHEST)
    expert_out = mixed.astype(jnp.bfloat16)
    return (attn_proj, expert_out)


def far_of(step, blk):
    return [(at, ((at // 2) ^ step) * 2 + at % 2) for at in range(blk)]


def side_of(size):
    return [(at, at ^ 1) for at in range(size)]


def place_of():
    blk_at = lax.axis_index("blk")
    return blk_at // 2, blk_at % 2


def grant(mebibytes):
    return pltpu.CompilerParams(vmem_limit_bytes=mebibytes << 20)


def in_vmem(count):
    return [pl.BlockSpec(memory_space=pltpu.VMEM)] * count


def prepare_kernel(sizes, *refs):
    far_count, span_length = sizes
    sources, (starts_hbm, ids_hbm, gates_hbm) = refs[:4], refs[4:7]
    targets, (pos_all, routes) = refs[7:11], refs[11:13]
    starts, ids_ref, gates_ref, sems = refs[13:]
    copies = [
        pltpu.make_async_copy(source, target, sems.at[at])
        for at, (source, target) in enumerate(
            zip((starts_hbm, ids_hbm, gates_hbm) + sources, (starts, ids_ref, gates_ref) + targets)
        )
    ]
    for copy in copies:
        copy.start()
    for copy in copies[:3]:
        copy.wait()
    _, near = place_of()
    tokens = pos_all.shape[0]
    piece = tokens // far_count
    for source in range(far_count):
        first = (source * 2 + near) * piece
        base = starts[first // span_length] + first % span_length
        pos_all[source * piece : (source + 1) * piece, :] = base + lax.broadcasted_iota(
            jnp.int32, (piece, HD), 0
        )
    gate_values = gates_ref[...].astype(jnp.float32)
    ids = ids_ref[...]
    route_weight = gate_values / jnp.sum(gate_values, axis=1, keepdims=True)
    own_tokens, top_count = gate_values.shape
    expert_lane = lax.broadcasted_iota(jnp.int32, (own_tokens, HD), 1) - HD // 2
    weight_of = jnp.zeros((own_tokens, HD), jnp.float32)
    for k in range(top_count):
        weight_of += jnp.where(expert_lane == ids[:, k : k + 1], route_weight[:, k : k + 1], 0.0)
    high = weight_of.astype(jnp.bfloat16).astype(jnp.float32)
    routes[...] = jnp.concatenate(
        [high, weight_of - high, jnp.zeros((tokens - 2 * own_tokens, HD), jnp.float32)], axis=0
    )
    for copy in copies[3:]:
        copy.wait()


def fetch_kernel(*refs):
    count = len(refs) // 2
    sems = refs[-1]
    copies = [
        pltpu.make_async_copy(refs[at], refs[count + at], sems.at[at]) for at in range(count)
    ]
    for copy in copies:
        copy.start()
    for copy in copies:
        copy.wait()


def attend_kernel(sizes, *refs):
    far_count, cache_rows, heads = sizes
    q_refs = refs[:far_count]
    key_own, key_side, value_own, value_side, pos_all, routes_ref = refs[far_count : far_count + 6]
    outs = refs[far_count + 6 : 2 * far_count + 6]
    q_all, keys, values, staged = refs[2 * far_count + 6 :]
    far, near = place_of()
    piece = q_refs[0].shape[0]
    tokens = far_count * piece
    own_heads = heads // far_count
    for step in range(far_count):
        source = far ^ step
        row = pl.multiple_of(source * piece, piece)
        for head in range(heads):
            q_all[pl.ds(head * tokens + row, piece), :] = q_refs[step][:, head * HD : (head + 1) * HD]
    keys[:cache_rows, :] = key_own[...]
    keys[cache_rows:, :] = key_side[...]
    values[:cache_rows, :] = value_own[...]
    values[cache_rows:, :] = value_side[...]
    lane_at = lax.broadcasted_iota(jnp.int32, (1, 2 * cache_rows), 1)
    own_first = (far * 2 + near) * cache_rows
    side_first = (far * 2 + 1 - near) * cache_rows - cache_rows
    key_pos = lane_at + jnp.where(lane_at < cache_rows, own_first, side_first)
    visible = key_pos <= pos_all[:, :1]
    routes = routes_ref[...]
    lane = lax.broadcasted_iota(jnp.int32, (tokens, HD), 1)
    scale = 1.0 / math.sqrt(HD)
    for group in range(far_count):
        rows = group * own_heads * tokens
        scores = lax.dot_general(
            q_all[rows : rows + own_heads * tokens, :],
            keys[...],
            (((1,), (1,)), ((), ())),
            preferred_element_type=jnp.float32,
        )
        extra = routes
        weights_16 = []
        for j in range(own_heads):
            part = jnp.where(visible, scores[j * tokens : (j + 1) * tokens] * scale, NEG_FILL)
            top = jnp.maximum(jnp.max(part, axis=1, keepdims=True), NEG_FILL / 10)
            top = top.astype(jnp.bfloat16).astype(jnp.float32)
            weights = jnp.exp(part - top)
            total = jnp.sum(weights, axis=1, keepdims=True)
            total_high = total.astype(jnp.bfloat16).astype(jnp.float32)
            extra = jnp.where(lane == 3 * j, top, extra)
            extra = jnp.where(lane == 3 * j + 1, total_high, extra)
            extra = jnp.where(lane == 3 * j + 2, total - total_high, extra)
            weights_16.append(weights.astype(jnp.bfloat16))
        numerator = jnp.dot(
            jnp.concatenate(weights_16, axis=0), values[...], preferred_element_type=jnp.float32
        ).astype(jnp.bfloat16)
        for j in range(own_heads):
            staged[group, :, j * HD : (j + 1) * HD] = numerator[j * tokens : (j + 1) * tokens]
        staged[group, :, own_heads * HD :] = extra.astype(jnp.bfloat16)
    for step in range(far_count):
        outs[step][...] = staged[far ^ step]


def project_kernel(sizes, *refs):
    far_count, own_heads, own_tokens = sizes
    messages = refs[:far_count]
    weight_own, weight_side, keep, send, routes, partial = refs[far_count:]
    far, near = place_of()
    row_at = lax.axis_index("rows")
    tokens = messages[0].shape[0]
    attended = []
    extras = [m[:, own_heads * HD :].astype(jnp.float32) for m in messages]
    for j in range(own_heads):
        tops = [e[:, 3 * j : 3 * j + 1] for e in extras]
        best = tops[0]
        for top in tops[1:]:
            best = jnp.maximum(best, top)
        above = jnp.zeros((tokens, HD), jnp.float32)
        below = jnp.zeros((tokens, 1), jnp.float32)
        for top, e, m in zip(tops, extras, messages):
            factor = jnp.exp(top - best)
            above += factor * m[:, j * HD : (j + 1) * HD].astype(jnp.float32)
            below += factor * (e[:, 3 * j + 1 : 3 * j + 2] + e[:, 3 * j + 2 : 3 * j + 3])
        attended.append(above / below)
    first = jnp.where(near == 0, attended[0], attended[1]).astype(jnp.bfloat16)
    second = jnp.where(near == 0, attended[1], attended[0]).astype(jnp.bfloat16)
    partial[...] = jnp.dot(
        first, weight_own[...], preferred_element_type=jnp.float32
    ) + jnp.dot(second, weight_side[...], preferred_element_type=jnp.float32)
    piece = tokens // far_count
    other = 1 - row_at
    mine, theirs = [], []
    for step in range(far_count):
        at = pl.multiple_of((far ^ step) * piece + row_at * own_tokens, own_tokens)
        mine.append(partial[pl.ds(at, own_tokens), :])
        at = pl.multiple_of((far ^ step) * piece + other * own_tokens, own_tokens)
        theirs.append(partial[pl.ds(at, own_tokens), :])
    keep[...] = jnp.concatenate(mine, axis=0)
    send[...] = jnp.concatenate(theirs, axis=0).astype(jnp.bfloat16)
    for at, step in enumerate(range(0, far_count, 2)):
        e = extras[step]
        routes[at * own_tokens : (at + 1) * own_tokens, :] = (
            e[:own_tokens] + e[own_tokens : 2 * own_tokens]
        )


def parts_kernel(keep, received, *outs):
    far_count = len(outs)
    own_tokens = keep.shape[0] // far_count
    total = keep[...] + received[...].astype(jnp.float32)
    blocks = [total[at * own_tokens : (at + 1) * own_tokens] for at in range(far_count)]
    for step, out in enumerate(outs):
        taken = [blocks[step ^ even] for even in range(0, far_count, 2)]
        out[...] = jnp.concatenate(taken, axis=0).astype(out.dtype)


def norm_kernel(far_count, *refs):
    parts = refs[:far_count]
    gain, routes, own_rows, spread = refs[far_count:]
    width = gain.shape[1]
    total = parts[0][...].astype(jnp.float32)
    for part in parts[1:]:
        total += part[...].astype(jnp.float32)
    rounded = total.astype(jnp.bfloat16)
    values_f = rounded.astype(jnp.float32)
    own_rows[...] = rounded[: own_rows.shape[0]]
    mean_square = jnp.mean(values_f * values_f, axis=1, keepdims=True)
    spread[:, :width] = (
        values_f * lax.rsqrt(mean_square + EPSILON) * gain[...].astype(jnp.float32)
    ).astype(jnp.bfloat16)
    weight_of = routes[...]
    high = weight_of.astype(jnp.bfloat16).astype(jnp.float32)
    low = pltpu.roll(weight_of - high, HD // 2, 1)
    high = pltpu.roll(high, HD // 2, 1)
    lane = lax.broadcasted_iota(jnp.int32, weight_of.shape, 1)
    spread[:, width:] = jnp.where(
        lane < HD // 2, high, pltpu.roll(low, HD // 2, 1)
    ).astype(jnp.bfloat16)


def expert_kernel(width, count, *refs):
    pieces = refs[:count]
    gate, up, down, keep, send, gathered, hidden = refs[count:]
    rows = pieces[0].shape[0]
    for at, piece in enumerate(pieces):
        gathered[at * rows : (at + 1) * rows, :] = piece[:, :width]
    arrived = gathered[...]
    ff = hidden.shape[1]
    chunk = math.gcd(ff, 256)
    for first in range(0, ff, chunk):
        gate_part = jnp.dot(
            arrived, gate[0, :, first : first + chunk], preferred_element_type=jnp.float32
        )
        up_part = jnp.dot(
            arrived, up[0, :, first : first + chunk], preferred_element_type=jnp.float32
        )
        hidden[:, first : first + chunk] = (
            gate_part / (1.0 + jnp.exp(-gate_part)) * up_part
        ).astype(jnp.bfloat16)
    expert = lax.axis_index("blk") * 2 + lax.axis_index("rows")
    lane = lax.broadcasted_iota(jnp.int32, (rows, HD), 1) % (HD // 2)
    shares = []
    for piece in pieces:
        routes = piece[:, width:].astype(jnp.float32)
        shares.append(jnp.sum(jnp.where(lane == expert, routes, 0.0), axis=1, keepdims=True))
    acted = hidden[...]
    for first in range(0, width, 512):
        last = min(first + 512, width)
        result = jnp.dot(acted, down[0, :, first:last], preferred_element_type=jnp.float32)
        result = result.astype(jnp.bfloat16).astype(jnp.float32)
        for at, share in enumerate(shares):
            target = keep if at < count // 2 else send
            half = at % (count // 2)
            target[half * rows : (half + 1) * rows, first:last] = (
                share * result[at * rows : (at + 1) * rows]
            ).astype(jnp.bfloat16)


def add_kernel(*refs):
    terms, out = refs[:-1], refs[-1]
    total = terms[0][...].astype(jnp.float32)
    for term in terms[1:]:
        total += term[...].astype(jnp.float32)
    out[...] = total.astype(out.dtype)


def quarters_kernel(keep, received, *outs):
    rows = outs[0].shape[0]
    for at, out in enumerate(outs):
        part = slice(at * rows, (at + 1) * rows)
        out[...] = (
            keep[part, :].astype(jnp.float32) + received[part, :].astype(jnp.float32)
        ).astype(out.dtype)


def last_kernel(*refs):
    terms, outs = refs[:4], refs[4:]
    rows = outs[0].shape[0]
    total = terms[0][...]
    for term in terms[1:]:
        total += term[...].astype(jnp.float32)
    for at, out in enumerate(outs):
        out[...] = total[at * rows : (at + 1) * rows].astype(out.dtype)


def paired_device(
    queries,
    cache_keys,
    cache_values,
    span_starts,
    out_weight,
    norm_gain,
    expert_ids,
    gate_fixed,
    gate_weight,
    up_weight,
    down_weight,
):
    blk, row_count = lax.axis_size("blk"), lax.axis_size("rows")
    far_count = blk // 2
    piece, query_width = queries.shape
    heads = query_width // HD
    own_heads = heads // far_count
    own_tokens = expert_ids.shape[0]
    tokens = far_count * piece
    held = far_count * own_tokens
    shared = held // 2
    width = out_weight.shape[1]
    cache_rows = cache_keys.shape[0]
    span_length = blk * piece // SPANS
    hidden = gate_weight.shape[2]
    bf16, f32 = jnp.bfloat16, jnp.float32
    shape_of = jax.ShapeDtypeStruct

    def over_far(arrays):
        moved = []
        for step in range(far_count - 1, 0, -1):
            moved.append(lax.ppermute(arrays[step], "blk", far_of(step, blk)))
        return [arrays[0]] + moved[::-1]

    def in_hbm(arrays):
        return [pltpu.with_memory_space_constraint(a, pltpu.HBM) for a in arrays]

    def fetched(*arrays):
        return pl.pallas_call(
            fetch_kernel,
            out_shape=[shape_of(a.shape, a.dtype) for a in arrays],
            in_specs=[pl.BlockSpec(memory_space=pltpu.HBM)] * len(arrays),
            out_specs=in_vmem(len(arrays)),
            scratch_shapes=[pltpu.SemaphoreType.DMA((len(arrays),))],
            compiler_params=grant(4),
        )(*in_hbm(arrays))

    def added(shape, dtype, *terms):
        return pl.pallas_call(
            add_kernel,
            out_shape=shape_of(shape, dtype),
            in_specs=in_vmem(len(terms)),
            out_specs=pl.BlockSpec(memory_space=pltpu.VMEM),
            compiler_params=grant(4),
            name="added",
        )(*terms)

    def over_close(arrays):
        moved = []
        for at, step in ((3, 3), (1, 1), (2, 2)):
            pairs = [(source, source ^ step) for source in range(blk)]
            moved.append(lax.ppermute(arrays[at], "blk", pairs))
        return [arrays[0], moved[1], moved[2], moved[0]]

    def over_near(array):
        return lax.ppermute(array, "blk", side_of(blk))

    def over_rows(array):
        return lax.ppermute(array, "rows", side_of(row_count))

    key_side = over_near(cache_keys)
    value_side = over_near(cache_values)
    q_pieces = over_far([queries] * far_count)
    weight_side = over_near(out_weight)
    local = [queries, cache_keys, cache_values, out_weight]
    *local, pos_all, routes = pl.pallas_call(
        functools.partial(prepare_kernel, (far_count, span_length)),
        out_shape=[shape_of(a.shape, a.dtype) for a in local]
        + [shape_of((tokens, HD), jnp.int32), shape_of((tokens, HD), f32)],
        in_specs=[pl.BlockSpec(memory_space=pltpu.HBM)] * 7,
        out_specs=in_vmem(6),
        scratch_shapes=[
            pltpu.SMEM(span_starts.shape, jnp.int32),
            pltpu.VMEM(expert_ids.shape, jnp.int32),
            pltpu.VMEM(gate_fixed.shape, jnp.int32),
            pltpu.SemaphoreType.DMA((7,)),
        ],
        compiler_params=grant(4),
        name="prepare",
    )(*in_hbm(local + [span_starts, expert_ids, gate_fixed]))
    queries_own, keys_own, values_own, weight_own = local
    q_pieces[0] = queries_own
    message_width = (own_heads + 1) * HD
    messages = pl.pallas_call(
        functools.partial(attend_kernel, (far_count, cache_rows, heads)),
        out_shape=[shape_of((tokens, message_width), bf16)] * far_count,
        in_specs=in_vmem(far_count + 6),
        out_specs=in_vmem(far_count),
        scratch_shapes=[
            pltpu.VMEM((heads * tokens, HD), bf16),
            pltpu.VMEM((2 * cache_rows, HD), bf16),
            pltpu.VMEM((2 * cache_rows, HD), bf16),
            pltpu.VMEM((far_count, tokens, message_width), bf16),
        ],
        compiler_params=grant(12),
        name="attend",
    )(*q_pieces, keys_own, key_side, values_own, value_side, pos_all, routes)
    messages = over_far(messages)
    (down_weight,) = fetched(down_weight)
    keep, send, routes = pl.pallas_call(
        functools.partial(project_kernel, (far_count, own_heads, own_tokens)),
        out_shape=[shape_of((held, width), f32), shape_of((held, width), bf16), shape_of((shared, HD), f32)],
        in_specs=in_vmem(far_count + 2),
        out_specs=in_vmem(3),
        scratch_shapes=[pltpu.VMEM((tokens, width), f32)],
        compiler_params=grant(8),
        name="project",
    )(*messages, weight_own, weight_side)
    parts = pl.pallas_call(
        parts_kernel,
        out_shape=[shape_of((shared, width), f32)] + [shape_of((shared, width), bf16)] * (far_count - 1),
        in_specs=in_vmem(2),
        out_specs=in_vmem(far_count),
        compiler_params=grant(4),
        name="parts",
    )(keep, over_rows(send))
    parts = over_far(parts)
    gate_weight, up_weight = fetched(gate_weight, up_weight)
    attn_proj, normed = pl.pallas_call(
        functools.partial(norm_kernel, far_count),
        out_shape=[shape_of((own_tokens, width), bf16), shape_of((shared, width + HD), bf16)],
        in_specs=in_vmem(far_count + 2),
        out_specs=in_vmem(2),
        compiler_params=grant(4),
        name="norm",
    )(*parts, norm_gain.reshape(1, width), routes)
    pieces = over_close([normed] * 4)
    pieces = pieces + [over_rows(piece) for piece in pieces]
    keep, send = pl.pallas_call(
        functools.partial(expert_kernel, width, len(pieces)),
        out_shape=[shape_of((4 * shared, width), bf16)] * 2,
        in_specs=in_vmem(len(pieces) + 3),
        out_specs=in_vmem(2),
        scratch_shapes=[
            pltpu.VMEM((len(pieces) * shared, width), bf16),
            pltpu.VMEM((len(pieces) * shared, hidden), bf16),
        ],
        compiler_params=grant(8),
        name="experts",
    )(*pieces, gate_weight, up_weight, down_weight)
    shares = pl.pallas_call(
        quarters_kernel,
        out_shape=[shape_of((shared, width), f32)] + [shape_of((shared, width), bf16)] * 3,
        in_specs=in_vmem(2),
        out_specs=in_vmem(4),
        compiler_params=grant(4),
        name="quarters",
    )(keep, over_rows(send))
    shares = over_close(shares)
    evens = list(range(0, far_count, 2))
    last = pl.pallas_call(
        last_kernel,
        out_shape=[shape_of((own_tokens, width), f32)]
        + [shape_of((own_tokens, width), bf16)] * (len(evens) - 1),
        in_specs=in_vmem(4),
        out_specs=in_vmem(len(evens)),
        compiler_params=grant(4),
        name="last",
    )(*shares)
    last = [last[0]] + [
        lax.ppermute(term, "blk", far_of(step, blk)) for term, step in zip(last[1:], evens[1:])
    ]
    return (attn_proj, added((own_tokens, width), bf16, *last))


def fits_pairs(mesh, queries, cache_keys, out_weight, expert_ids, gate_weight):
    blk, row_count = mesh.shape["blk"], mesh.shape["rows"]
    parts = mesh.shape["groups"]
    far_count = blk // 2
    if blk % 2 or row_count != 2 or far_count < 2 or far_count & (far_count - 1):
        return False
    heads = queries.shape[1] // (row_count * HD)
    piece = queries.shape[0] // (parts * blk)
    own_tokens = expert_ids.shape[0] // (parts * blk * row_count)
    experts = gate_weight.shape[0]
    return (
        cache_keys.shape[1] == row_count * HD
        and heads == 2 * far_count
        and out_weight.shape[0] == row_count * blk * HD
        and out_weight.shape[1] % HD == 0
        and piece == 2 * own_tokens
        and own_tokens % 8 == 0
        and (blk * piece // SPANS) % piece == 0
        and experts == blk * row_count
        and experts <= HD // 2
        and gate_weight.shape[2] % 128 == 0
    )


def solution(mesh):
    in_specs = (
        P(("groups", "blk"), "rows"),
        P(("groups", "blk"), "rows"),
        P(("groups", "blk"), "rows"),
        P("groups"),
        P(("rows", "blk"), None),
        P(),
        P(("groups", "blk", "rows"), None),
        P(("groups", "blk", "rows"), None),
        P(("blk", "rows"), None, None),
        P(("blk", "rows"), None, None),
        P(("blk", "rows"), None, None),
    )
    out_specs = (P(("groups", "blk", "rows"), None), P(("groups", "blk", "rows"), None))

    def mapped(body):
        return jax.shard_map(
            body, mesh=mesh, in_specs=in_specs, out_specs=out_specs, check_vma=False
        )

    def run(*arrays):
        queries, cache_keys, out_weight = arrays[0], arrays[1], arrays[4]
        expert_ids, gate_weight = arrays[6], arrays[8]
        if not fits_pairs(mesh, queries, cache_keys, out_weight, expert_ids, gate_weight):
            return mapped(on_device)(*arrays)
        return mapped(paired_device)(*arrays)

    return run
```

```python
import functools
import math

import jax
import jax.numpy as jnp
from jax import lax
from jax.experimental import pallas as pl
from jax.experimental.pallas import tpu as pltpu
from jax.sharding import PartitionSpec as P


HD = 128
SPANS = 2


NEG_FILL = -1e30
EPSILON = 1e-06


def partial_attention(query_block, query_pos, cache_keys, cache_values, key_pos):
    rows_here = query_block.shape[0]
    kv_local = cache_keys.shape[1] // HD
    group_size = query_block.shape[1] // (kv_local * HD)
    heads_here = kv_local * group_size
    shaped_q = query_block.reshape(rows_here, kv_local, group_size, HD)
    shaped_k = cache_keys.reshape(-1, kv_local, HD)
    shaped_v = cache_values.reshape(-1, kv_local, HD)
    scores = jnp.einsum(
        "qgjd,kgd->qgjk", shaped_q, shaped_k, preferred_element_type=jnp.float32
    ) * (1.0 / math.sqrt(HD))
    visible = (key_pos[None, :] <= query_pos[:, None])[:, None, None, :]
    scores = jnp.where(visible, scores, NEG_FILL)
    row_top = jnp.max(scores, axis=-1)
    weights = jnp.where(visible, jnp.exp(scores - row_top[..., None]), 0.0)
    totals = jnp.sum(weights, axis=-1)
    numerator = jnp.einsum(
        "qgjk,kgd->qgjd", weights.astype(jnp.bfloat16), shaped_v, preferred_element_type=jnp.float32
    )
    return (
        row_top.reshape(rows_here, heads_here),
        totals.reshape(rows_here, heads_here),
        numerator.reshape(rows_here, heads_here * HD),
    )


def run_experts(arrived, gate_weight, up_weight, down_weight):
    gate_part = jnp.einsum(
        "secd,edf->secf", arrived, gate_weight, preferred_element_type=jnp.float32
    )
    up_part = jnp.einsum("secd,edf->secf", arrived, up_weight, preferred_element_type=jnp.float32)
    hidden = (jax.nn.silu(gate_part) * up_part).astype(jnp.bfloat16)
    return jnp.einsum(
        "secf,efd->secd", hidden, down_weight, preferred_element_type=jnp.float32
    ).astype(jnp.bfloat16)


def on_device(
    queries,
    cache_keys,
    cache_values,
    span_starts,
    out_weight,
    norm_gain,
    expert_ids,
    gate_fixed,
    gate_weight,
    up_weight,
    down_weight,
):
    gathered = lax.all_gather(queries, "blk", axis=0, tiled=True)
    total_rows = gathered.shape[0]
    width = gathered.shape[1]
    span_length = total_rows // SPANS
    token_index = jnp.arange(total_rows, dtype=jnp.int32)
    span_index = token_index // span_length
    span_match = span_index[:, None] == jnp.arange(SPANS, dtype=jnp.int32)[None, :]
    start_of = jnp.sum(jnp.where(span_match, span_starts[None, :], 0), axis=1)
    query_pos = start_of + token_index % span_length
    cache_rows = cache_keys.shape[0]
    key_pos = lax.axis_index("blk") * cache_rows + jnp.arange(cache_rows, dtype=jnp.int32)
    block_rows = math.gcd(total_rows, 128)
    block_count = total_rows // block_rows

    def one_block(item):
        return partial_attention(item[0], item[1], cache_keys, cache_values, key_pos)

    blocked = (
        gathered.reshape(block_count, block_rows, width),
        query_pos.reshape(block_count, block_rows),
    )
    row_top, totals, numerator = lax.map(one_block, blocked)
    heads_here = row_top.shape[2]
    row_top = row_top.reshape(total_rows, heads_here)
    totals = totals.reshape(total_rows, heads_here)
    numerator = numerator.reshape(total_rows, heads_here * HD)
    global_top = lax.pmax(row_top, "blk")
    factor = jnp.exp(row_top - global_top)
    totals = totals * factor
    numerator = (numerator.reshape(total_rows, heads_here, HD) * factor[:, :, None]).reshape(
        total_rows, heads_here * HD
    )
    own_numer = lax.psum_scatter(
        numerator.astype(jnp.bfloat16), "blk", scatter_dimension=1, tiled=True
    ).astype(jnp.float32)
    all_totals = lax.psum(totals, "blk")
    col_width = own_numer.shape[1]
    first_col = lax.axis_index("blk") * col_width
    spread = jnp.repeat(all_totals, HD, axis=1)
    col_totals = lax.dynamic_slice_in_dim(spread, first_col, col_width, 1)
    attended = (own_numer / col_totals).astype(jnp.bfloat16)
    projected = lax.psum_scatter(
        jnp.dot(attended, out_weight, preferred_element_type=jnp.float32),
        ("blk", "rows"),
        scatter_dimension=0,
        tiled=True,
    )
    attn_proj = projected.astype(jnp.bfloat16)
    values_f = attn_proj.astype(jnp.float32)
    mean_square = jnp.mean(values_f * values_f, axis=-1, keepdims=True)
    normed = (values_f * lax.rsqrt(mean_square + EPSILON) * norm_gain.astype(jnp.float32)).astype(
        jnp.bfloat16
    )
    own_tokens = normed.shape[0]
    top_count = expert_ids.shape[1]
    owners = lax.axis_size("blk") * lax.axis_size("rows")
    local_experts = gate_weight.shape[0]
    expert_count = owners * local_experts
    capacity = min(own_tokens, max(2, 2 * top_count * own_tokens // expert_count))
    slot_total = expert_count * capacity
    route_expert = expert_ids.reshape(-1)
    route_count = route_expert.shape[0]
    hits = (route_expert[:, None] == jnp.arange(expert_count, dtype=jnp.int32)[None, :]).astype(
        jnp.int32
    )
    slot_number = jnp.sum(jnp.cumsum(hits, axis=0) * hits, axis=1) - 1
    target = route_expert * capacity + slot_number
    placed = target[:, None] == jnp.arange(slot_total, dtype=jnp.int32)[None, :]
    route_token = jnp.arange(route_count, dtype=jnp.int32) // top_count
    token_pick = route_token[:, None] == jnp.arange(own_tokens, dtype=jnp.int32)[None, :]
    slot_token = jnp.dot(
        placed.astype(jnp.bfloat16).T,
        token_pick.astype(jnp.bfloat16),
        preferred_element_type=jnp.float32,
    ).astype(jnp.bfloat16)
    outgoing = jnp.dot(slot_token, normed, preferred_element_type=jnp.float32).astype(jnp.bfloat16)
    outgoing = outgoing.reshape(owners, local_experts, capacity, -1)
    gate_values = gate_fixed.astype(jnp.float32)
    route_weight = (gate_values / jnp.sum(gate_values, axis=1, keepdims=True)).reshape(-1)
    weighted_pick = token_pick.astype(jnp.float32) * route_weight[:, None]
    blend = jnp.dot(weighted_pick.T, placed.astype(jnp.float32), precision=lax.Precision.HIGHEST)
    finished = run_experts(
        lax.all_to_all(outgoing, ("blk", "rows"), split_axis=0, concat_axis=0, tiled=True),
        gate_weight,
        up_weight,
        down_weight,
    )
    returned = lax.all_to_all(finished, ("blk", "rows"), split_axis=0, concat_axis=0, tiled=True)
    returned_flat = returned.reshape(slot_total, -1)
    mixed = jnp.dot(blend, returned_flat.astype(jnp.float32), precision=lax.Precision.HIGHEST)
    expert_out = mixed.astype(jnp.bfloat16)
    return (attn_proj, expert_out)


def far_of(step, blk):
    return [(at, ((at // 2) ^ step) * 2 + at % 2) for at in range(blk)]


def side_of(size):
    return [(at, at ^ 1) for at in range(size)]


def place_of():
    blk_at = lax.axis_index("blk")
    return blk_at // 2, blk_at % 2


def grant(mebibytes):
    return pltpu.CompilerParams(vmem_limit_bytes=mebibytes << 20)


def in_vmem(count):
    return [pl.BlockSpec(memory_space=pltpu.VMEM)] * count


def prepare_kernel(sizes, *refs):
    far_count, span_length = sizes
    sources, (starts_hbm, ids_hbm, gates_hbm) = refs[:4], refs[4:7]
    targets, (pos_all, routes) = refs[7:11], refs[11:13]
    starts, ids_ref, gates_ref, sems = refs[13:]
    copies = [
        pltpu.make_async_copy(source, target, sems.at[at])
        for at, (source, target) in enumerate(
            zip((starts_hbm, ids_hbm, gates_hbm) + sources, (starts, ids_ref, gates_ref) + targets)
        )
    ]
    for copy in copies:
        copy.start()
    for copy in copies[:3]:
        copy.wait()
    _, near = place_of()
    tokens = pos_all.shape[0]
    piece = tokens // far_count
    for source in range(far_count):
        first = (source * 2 + near) * piece
        base = starts[first // span_length] + first % span_length
        pos_all[source * piece : (source + 1) * piece, :] = base + lax.broadcasted_iota(
            jnp.int32, (piece, HD), 0
        )
    gate_values = gates_ref[...].astype(jnp.float32)
    ids = ids_ref[...]
    route_weight = gate_values / jnp.sum(gate_values, axis=1, keepdims=True)
    own_tokens, top_count = gate_values.shape
    expert_lane = lax.broadcasted_iota(jnp.int32, (own_tokens, HD), 1) - HD // 2
    weight_of = jnp.zeros((own_tokens, HD), jnp.float32)
    for k in range(top_count):
        weight_of += jnp.where(expert_lane == ids[:, k : k + 1], route_weight[:, k : k + 1], 0.0)
    high = weight_of.astype(jnp.bfloat16).astype(jnp.float32)
    routes[...] = jnp.concatenate(
        [high, weight_of - high, jnp.zeros((tokens - 2 * own_tokens, HD), jnp.float32)], axis=0
    )
    for copy in copies[3:]:
        copy.wait()


def fetch_kernel(*refs):
    count = len(refs) // 2
    sems = refs[-1]
    copies = [
        pltpu.make_async_copy(refs[at], refs[count + at], sems.at[at]) for at in range(count)
    ]
    for copy in copies:
        copy.start()
    for copy in copies:
        copy.wait()


def attend_kernel(sizes, *refs):
    far_count, cache_rows, heads = sizes
    q_refs = refs[:far_count]
    key_own, key_side, value_own, value_side, pos_all, routes_ref = refs[far_count : far_count + 6]
    outs = refs[far_count + 6 : 2 * far_count + 6]
    q_all, keys, values, staged = refs[2 * far_count + 6 :]
    far, near = place_of()
    piece = q_refs[0].shape[0]
    tokens = far_count * piece
    own_heads = heads // far_count
    for step in range(far_count):
        source = far ^ step
        row = pl.multiple_of(source * piece, piece)
        for head in range(heads):
            q_all[pl.ds(head * tokens + row, piece), :] = q_refs[step][:, head * HD : (head + 1) * HD]
    keys[:cache_rows, :] = key_own[...]
    keys[cache_rows:, :] = key_side[...]
    values[:cache_rows, :] = value_own[...]
    values[cache_rows:, :] = value_side[...]
    lane_at = lax.broadcasted_iota(jnp.int32, (1, 2 * cache_rows), 1)
    own_first = (far * 2 + near) * cache_rows
    side_first = (far * 2 + 1 - near) * cache_rows - cache_rows
    key_pos = lane_at + jnp.where(lane_at < cache_rows, own_first, side_first)
    visible = key_pos <= pos_all[:, :1]
    routes = routes_ref[...]
    lane = lax.broadcasted_iota(jnp.int32, (tokens, HD), 1)
    scale = 1.0 / math.sqrt(HD)
    for group in range(far_count):
        rows = group * own_heads * tokens
        scores = lax.dot_general(
            q_all[rows : rows + own_heads * tokens, :],
            keys[...],
            (((1,), (1,)), ((), ())),
            preferred_element_type=jnp.float32,
        )
        extra = routes
        weights_16 = []
        for j in range(own_heads):
            part = jnp.where(visible, scores[j * tokens : (j + 1) * tokens] * scale, NEG_FILL)
            top = jnp.maximum(jnp.max(part, axis=1, keepdims=True), NEG_FILL / 10)
            top = top.astype(jnp.bfloat16).astype(jnp.float32)
            weights = jnp.exp(part - top)
            total = jnp.sum(weights, axis=1, keepdims=True)
            total_high = total.astype(jnp.bfloat16).astype(jnp.float32)
            extra = jnp.where(lane == 3 * j, top, extra)
            extra = jnp.where(lane == 3 * j + 1, total_high, extra)
            extra = jnp.where(lane == 3 * j + 2, total - total_high, extra)
            weights_16.append(weights.astype(jnp.bfloat16))
        numerator = jnp.dot(
            jnp.concatenate(weights_16, axis=0), values[...], preferred_element_type=jnp.float32
        ).astype(jnp.bfloat16)
        for j in range(own_heads):
            staged[group, :, j * HD : (j + 1) * HD] = numerator[j * tokens : (j + 1) * tokens]
        staged[group, :, own_heads * HD :] = extra.astype(jnp.bfloat16)
    for step in range(far_count):
        outs[step][...] = staged[far ^ step]


def project_kernel(sizes, *refs):
    far_count, own_heads, own_tokens = sizes
    messages = refs[:far_count]
    weight_own, weight_side, keep, send, routes, partial = refs[far_count:]
    far, near = place_of()
    row_at = lax.axis_index("rows")
    tokens = messages[0].shape[0]
    attended = []
    extras = [m[:, own_heads * HD :].astype(jnp.float32) for m in messages]
    for j in range(own_heads):
        tops = [e[:, 3 * j : 3 * j + 1] for e in extras]
        best = tops[0]
        for top in tops[1:]:
            best = jnp.maximum(best, top)
        above = jnp.zeros((tokens, HD), jnp.float32)
        below = jnp.zeros((tokens, 1), jnp.float32)
        for top, e, m in zip(tops, extras, messages):
            factor = jnp.exp(top - best)
            above += factor * m[:, j * HD : (j + 1) * HD].astype(jnp.float32)
            below += factor * (e[:, 3 * j + 1 : 3 * j + 2] + e[:, 3 * j + 2 : 3 * j + 3])
        attended.append(above / below)
    first = jnp.where(near == 0, attended[0], attended[1]).astype(jnp.bfloat16)
    second = jnp.where(near == 0, attended[1], attended[0]).astype(jnp.bfloat16)
    partial[...] = jnp.dot(
        first, weight_own[...], preferred_element_type=jnp.float32
    ) + jnp.dot(second, weight_side[...], preferred_element_type=jnp.float32)
    piece = tokens // far_count
    other = 1 - row_at
    mine, theirs = [], []
    for step in range(far_count):
        at = pl.multiple_of((far ^ step) * piece + row_at * own_tokens, own_tokens)
        mine.append(partial[pl.ds(at, own_tokens), :])
        at = pl.multiple_of((far ^ step) * piece + other * own_tokens, own_tokens)
        theirs.append(partial[pl.ds(at, own_tokens), :])
    keep[...] = jnp.concatenate(mine, axis=0)
    send[...] = jnp.concatenate(theirs, axis=0).astype(jnp.bfloat16)
    for at, step in enumerate(range(0, far_count, 2)):
        e = extras[step]
        routes[at * own_tokens : (at + 1) * own_tokens, :] = (
            e[:own_tokens] + e[own_tokens : 2 * own_tokens]
        )


def parts_kernel(keep, received, *outs):
    far_count = len(outs)
    own_tokens = keep.shape[0] // far_count
    total = keep[...] + received[...].astype(jnp.float32)
    blocks = [total[at * own_tokens : (at + 1) * own_tokens] for at in range(far_count)]
    for step, out in enumerate(outs):
        taken = [blocks[step ^ even] for even in range(0, far_count, 2)]
        out[...] = jnp.concatenate(taken, axis=0).astype(out.dtype)


def norm_kernel(far_count, *refs):
    parts = refs[:far_count]
    gain, routes, own_rows, spread = refs[far_count:]
    width = gain.shape[1]
    total = parts[0][...].astype(jnp.float32)
    for part in parts[1:]:
        total += part[...].astype(jnp.float32)
    rounded = total.astype(jnp.bfloat16)
    values_f = rounded.astype(jnp.float32)
    own_rows[...] = rounded[: own_rows.shape[0]]
    mean_square = jnp.mean(values_f * values_f, axis=1, keepdims=True)
    spread[:, :width] = (
        values_f * lax.rsqrt(mean_square + EPSILON) * gain[...].astype(jnp.float32)
    ).astype(jnp.bfloat16)
    weight_of = routes[...]
    high = weight_of.astype(jnp.bfloat16).astype(jnp.float32)
    low = pltpu.roll(weight_of - high, HD // 2, 1)
    high = pltpu.roll(high, HD // 2, 1)
    lane = lax.broadcasted_iota(jnp.int32, weight_of.shape, 1)
    spread[:, width:] = jnp.where(
        lane < HD // 2, high, pltpu.roll(low, HD // 2, 1)
    ).astype(jnp.bfloat16)


def expert_kernel(width, count, *refs):
    pieces = refs[:count]
    gate, up, down, keep, send, gathered, hidden = refs[count:]
    rows = pieces[0].shape[0]
    for at, piece in enumerate(pieces):
        gathered[at * rows : (at + 1) * rows, :] = piece[:, :width]
    arrived = gathered[...]
    ff = hidden.shape[1]
    chunk = math.gcd(ff, 256)
    for first in range(0, ff, chunk):
        gate_part = jnp.dot(
            arrived, gate[0, :, first : first + chunk], preferred_element_type=jnp.float32
        )
        up_part = jnp.dot(
            arrived, up[0, :, first : first + chunk], preferred_element_type=jnp.float32
        )
        hidden[:, first : first + chunk] = (
            gate_part / (1.0 + jnp.exp(-gate_part)) * up_part
        ).astype(jnp.bfloat16)
    expert = lax.axis_index("blk") * 2 + lax.axis_index("rows")
    lane = lax.broadcasted_iota(jnp.int32, (rows, HD), 1) % (HD // 2)
    shares = []
    for piece in pieces:
        routes = piece[:, width:].astype(jnp.float32)
        shares.append(jnp.sum(jnp.where(lane == expert, routes, 0.0), axis=1, keepdims=True))
    acted = hidden[...]
    for first in range(0, width, 512):
        last = min(first + 512, width)
        result = jnp.dot(acted, down[0, :, first:last], preferred_element_type=jnp.float32)
        result = result.astype(jnp.bfloat16).astype(jnp.float32)
        for at, share in enumerate(shares):
            target = keep if at < count // 2 else send
            half = at % (count // 2)
            target[half * rows : (half + 1) * rows, first:last] = (
                share * result[at * rows : (at + 1) * rows]
            ).astype(jnp.bfloat16)


def add_kernel(*refs):
    terms, out = refs[:-1], refs[-1]
    total = terms[0][...].astype(jnp.float32)
    for term in terms[1:]:
        total += term[...].astype(jnp.float32)
    out[...] = total.astype(out.dtype)


def quarters_kernel(keep, received, *outs):
    rows = outs[0].shape[0]
    for at, out in enumerate(outs):
        part = slice(at * rows, (at + 1) * rows)
        out[...] = (
            keep[part, :].astype(jnp.float32) + received[part, :].astype(jnp.float32)
        ).astype(out.dtype)


def last_kernel(*refs):
    terms, outs = refs[:4], refs[4:]
    rows = outs[0].shape[0]
    total = terms[0][...]
    for term in terms[1:]:
        total += term[...].astype(jnp.float32)
    for at, out in enumerate(outs):
        out[...] = total[at * rows : (at + 1) * rows].astype(out.dtype)


def paired_device(
    queries,
    cache_keys,
    cache_values,
    span_starts,
    out_weight,
    norm_gain,
    expert_ids,
    gate_fixed,
    gate_weight,
    up_weight,
    down_weight,
):
    blk, row_count = lax.axis_size("blk"), lax.axis_size("rows")
    far_count = blk // 2
    piece, query_width = queries.shape
    heads = query_width // HD
    own_heads = heads // far_count
    own_tokens = expert_ids.shape[0]
    tokens = far_count * piece
    held = far_count * own_tokens
    shared = held // 2
    width = out_weight.shape[1]
    cache_rows = cache_keys.shape[0]
    span_length = blk * piece // SPANS
    hidden = gate_weight.shape[2]
    bf16, f32 = jnp.bfloat16, jnp.float32
    shape_of = jax.ShapeDtypeStruct

    def over_far(arrays):
        moved = [arrays[0]]
        for step in range(1, far_count):
            moved.append(lax.ppermute(arrays[step], "blk", far_of(step, blk)))
        return moved

    def in_hbm(arrays):
        return [pltpu.with_memory_space_constraint(a, pltpu.HBM) for a in arrays]

    def fetched(*arrays):
        return pl.pallas_call(
            fetch_kernel,
            out_shape=[shape_of(a.shape, a.dtype) for a in arrays],
            in_specs=[pl.BlockSpec(memory_space=pltpu.HBM)] * len(arrays),
            out_specs=in_vmem(len(arrays)),
            scratch_shapes=[pltpu.SemaphoreType.DMA((len(arrays),))],
            compiler_params=grant(4),
        )(*in_hbm(arrays))

    def added(shape, dtype, *terms):
        return pl.pallas_call(
            add_kernel,
            out_shape=shape_of(shape, dtype),
            in_specs=in_vmem(len(terms)),
            out_specs=pl.BlockSpec(memory_space=pltpu.VMEM),
            compiler_params=grant(4),
            name="added",
        )(*terms)

    def over_close(arrays):
        moved = [arrays[0]]
        for step in range(1, 4):
            pairs = [(source, source ^ step) for source in range(blk)]
            moved.append(lax.ppermute(arrays[step], "blk", pairs))
        return moved

    def over_near(array):
        return lax.ppermute(array, "blk", side_of(blk))

    def over_rows(array):
        return lax.ppermute(array, "rows", side_of(row_count))

    key_side = over_near(cache_keys)
    value_side = over_near(cache_values)
    q_pieces = over_far([queries] * far_count)
    weight_side = over_near(out_weight)
    local = [queries, cache_keys, cache_values, out_weight]
    *local, pos_all, routes = pl.pallas_call(
        functools.partial(prepare_kernel, (far_count, span_length)),
        out_shape=[shape_of(a.shape, a.dtype) for a in local]
        + [shape_of((tokens, HD), jnp.int32), shape_of((tokens, HD), f32)],
        in_specs=[pl.BlockSpec(memory_space=pltpu.HBM)] * 7,
        out_specs=in_vmem(6),
        scratch_shapes=[
            pltpu.SMEM(span_starts.shape, jnp.int32),
            pltpu.VMEM(expert_ids.shape, jnp.int32),
            pltpu.VMEM(gate_fixed.shape, jnp.int32),
            pltpu.SemaphoreType.DMA((7,)),
        ],
        compiler_params=grant(4),
        name="prepare",
    )(*in_hbm(local + [span_starts, expert_ids, gate_fixed]))
    queries_own, keys_own, values_own, weight_own = local
    q_pieces[0] = queries_own
    message_width = (own_heads + 1) * HD
    messages = pl.pallas_call(
        functools.partial(attend_kernel, (far_count, cache_rows, heads)),
        out_shape=[shape_of((tokens, message_width), bf16)] * far_count,
        in_specs=in_vmem(far_count + 6),
        out_specs=in_vmem(far_count),
        scratch_shapes=[
            pltpu.VMEM((heads * tokens, HD), bf16),
            pltpu.VMEM((2 * cache_rows, HD), bf16),
            pltpu.VMEM((2 * cache_rows, HD), bf16),
            pltpu.VMEM((far_count, tokens, message_width), bf16),
        ],
        compiler_params=grant(12),
        name="attend",
    )(*q_pieces, keys_own, key_side, values_own, value_side, pos_all, routes)
    messages = over_far(messages)
    (down_weight,) = fetched(down_weight)
    keep, send, routes = pl.pallas_call(
        functools.partial(project_kernel, (far_count, own_heads, own_tokens)),
        out_shape=[shape_of((held, width), f32), shape_of((held, width), bf16), shape_of((shared, HD), f32)],
        in_specs=in_vmem(far_count + 2),
        out_specs=in_vmem(3),
        scratch_shapes=[pltpu.VMEM((tokens, width), f32)],
        compiler_params=grant(8),
        name="project",
    )(*messages, weight_own, weight_side)
    parts = pl.pallas_call(
        parts_kernel,
        out_shape=[shape_of((shared, width), f32)] + [shape_of((shared, width), bf16)] * (far_count - 1),
        in_specs=in_vmem(2),
        out_specs=in_vmem(far_count),
        compiler_params=grant(4),
        name="parts",
    )(keep, over_rows(send))
    parts = over_far(parts)
    gate_weight, up_weight = fetched(gate_weight, up_weight)
    attn_proj, normed = pl.pallas_call(
        functools.partial(norm_kernel, far_count),
        out_shape=[pltpu.VMEM((own_tokens, width), bf16), shape_of((shared, width + HD), bf16)],
        in_specs=in_vmem(far_count + 2),
        out_specs=in_vmem(2),
        compiler_params=grant(4),
        name="norm",
    )(*parts, norm_gain.reshape(1, width), routes)
    pieces = over_close([normed] * 4)
    attn_proj = pl.pallas_call(
        add_kernel,
        out_shape=shape_of((own_tokens, width), bf16),
        in_specs=in_vmem(1),
        out_specs=pl.BlockSpec(memory_space=pltpu.VMEM),
        compiler_params=grant(4),
        name="emit",
    )(attn_proj)
    pieces = pieces + [over_rows(piece) for piece in pieces]
    keep, send = pl.pallas_call(
        functools.partial(expert_kernel, width, len(pieces)),
        out_shape=[shape_of((4 * shared, width), bf16)] * 2,
        in_specs=in_vmem(len(pieces) + 3),
        out_specs=in_vmem(2),
        scratch_shapes=[
            pltpu.VMEM((len(pieces) * shared, width), bf16),
            pltpu.VMEM((len(pieces) * shared, hidden), bf16),
        ],
        compiler_params=grant(8),
        name="experts",
    )(*pieces, gate_weight, up_weight, down_weight)
    shares = pl.pallas_call(
        quarters_kernel,
        out_shape=[shape_of((shared, width), f32)] + [shape_of((shared, width), bf16)] * 3,
        in_specs=in_vmem(2),
        out_specs=in_vmem(4),
        compiler_params=grant(4),
        name="quarters",
    )(keep, over_rows(send))
    shares = over_close(shares)
    evens = list(range(0, far_count, 2))
    last = pl.pallas_call(
        last_kernel,
        out_shape=[shape_of((own_tokens, width), f32)]
        + [shape_of((own_tokens, width), bf16)] * (len(evens) - 1),
        in_specs=in_vmem(4),
        out_specs=in_vmem(len(evens)),
        compiler_params=grant(4),
        name="last",
    )(*shares)
    last = [last[0]] + [
        lax.ppermute(term, "blk", far_of(step, blk)) for term, step in zip(last[1:], evens[1:])
    ]
    return (attn_proj, added((own_tokens, width), bf16, *last))


def fits_pairs(mesh, queries, cache_keys, out_weight, expert_ids, gate_weight):
    blk, row_count = mesh.shape["blk"], mesh.shape["rows"]
    parts = mesh.shape["groups"]
    far_count = blk // 2
    if blk % 2 or row_count != 2 or far_count < 2 or far_count & (far_count - 1):
        return False
    heads = queries.shape[1] // (row_count * HD)
    piece = queries.shape[0] // (parts * blk)
    own_tokens = expert_ids.shape[0] // (parts * blk * row_count)
    experts = gate_weight.shape[0]
    return (
        cache_keys.shape[1] == row_count * HD
        and heads == 2 * far_count
        and out_weight.shape[0] == row_count * blk * HD
        and out_weight.shape[1] % HD == 0
        and piece == 2 * own_tokens
        and own_tokens % 8 == 0
        and (blk * piece // SPANS) % piece == 0
        and experts == blk * row_count
        and experts <= HD // 2
        and gate_weight.shape[2] % 128 == 0
    )


def solution(mesh):
    in_specs = (
        P(("groups", "blk"), "rows"),
        P(("groups", "blk"), "rows"),
        P(("groups", "blk"), "rows"),
        P("groups"),
        P(("rows", "blk"), None),
        P(),
        P(("groups", "blk", "rows"), None),
        P(("groups", "blk", "rows"), None),
        P(("blk", "rows"), None, None),
        P(("blk", "rows"), None, None),
        P(("blk", "rows"), None, None),
    )
    out_specs = (P(("groups", "blk", "rows"), None), P(("groups", "blk", "rows"), None))

    def mapped(body):
        return jax.shard_map(
            body, mesh=mesh, in_specs=in_specs, out_specs=out_specs, check_vma=False
        )

    def run(*arrays):
        queries, cache_keys, out_weight = arrays[0], arrays[1], arrays[4]
        expert_ids, gate_weight = arrays[6], arrays[8]
        if not fits_pairs(mesh, queries, cache_keys, out_weight, expert_ids, gate_weight):
            return mapped(on_device)(*arrays)
        return mapped(paired_device)(*arrays)

    return run
```

```python
import functools
import math

import jax
import jax.numpy as jnp
from jax import lax
from jax.experimental import pallas as pl
from jax.experimental.pallas import tpu as pltpu
from jax.sharding import PartitionSpec as P


HD = 128
SPANS = 2


NEG_FILL = -1e30
EPSILON = 1e-06


def partial_attention(query_block, query_pos, cache_keys, cache_values, key_pos):
    rows_here = query_block.shape[0]
    kv_local = cache_keys.shape[1] // HD
    group_size = query_block.shape[1] // (kv_local * HD)
    heads_here = kv_local * group_size
    shaped_q = query_block.reshape(rows_here, kv_local, group_size, HD)
    shaped_k = cache_keys.reshape(-1, kv_local, HD)
    shaped_v = cache_values.reshape(-1, kv_local, HD)
    scores = jnp.einsum(
        "qgjd,kgd->qgjk", shaped_q, shaped_k, preferred_element_type=jnp.float32
    ) * (1.0 / math.sqrt(HD))
    visible = (key_pos[None, :] <= query_pos[:, None])[:, None, None, :]
    scores = jnp.where(visible, scores, NEG_FILL)
    row_top = jnp.max(scores, axis=-1)
    weights = jnp.where(visible, jnp.exp(scores - row_top[..., None]), 0.0)
    totals = jnp.sum(weights, axis=-1)
    numerator = jnp.einsum(
        "qgjk,kgd->qgjd", weights.astype(jnp.bfloat16), shaped_v, preferred_element_type=jnp.float32
    )
    return (
        row_top.reshape(rows_here, heads_here),
        totals.reshape(rows_here, heads_here),
        numerator.reshape(rows_here, heads_here * HD),
    )


def run_experts(arrived, gate_weight, up_weight, down_weight):
    gate_part = jnp.einsum(
        "secd,edf->secf", arrived, gate_weight, preferred_element_type=jnp.float32
    )
    up_part = jnp.einsum("secd,edf->secf", arrived, up_weight, preferred_element_type=jnp.float32)
    hidden = (jax.nn.silu(gate_part) * up_part).astype(jnp.bfloat16)
    return jnp.einsum(
        "secf,efd->secd", hidden, down_weight, preferred_element_type=jnp.float32
    ).astype(jnp.bfloat16)


def on_device(
    queries,
    cache_keys,
    cache_values,
    span_starts,
    out_weight,
    norm_gain,
    expert_ids,
    gate_fixed,
    gate_weight,
    up_weight,
    down_weight,
):
    gathered = lax.all_gather(queries, "blk", axis=0, tiled=True)
    total_rows = gathered.shape[0]
    width = gathered.shape[1]
    span_length = total_rows // SPANS
    token_index = jnp.arange(total_rows, dtype=jnp.int32)
    span_index = token_index // span_length
    span_match = span_index[:, None] == jnp.arange(SPANS, dtype=jnp.int32)[None, :]
    start_of = jnp.sum(jnp.where(span_match, span_starts[None, :], 0), axis=1)
    query_pos = start_of + token_index % span_length
    cache_rows = cache_keys.shape[0]
    key_pos = lax.axis_index("blk") * cache_rows + jnp.arange(cache_rows, dtype=jnp.int32)
    block_rows = math.gcd(total_rows, 128)
    block_count = total_rows // block_rows

    def one_block(item):
        return partial_attention(item[0], item[1], cache_keys, cache_values, key_pos)

    blocked = (
        gathered.reshape(block_count, block_rows, width),
        query_pos.reshape(block_count, block_rows),
    )
    row_top, totals, numerator = lax.map(one_block, blocked)
    heads_here = row_top.shape[2]
    row_top = row_top.reshape(total_rows, heads_here)
    totals = totals.reshape(total_rows, heads_here)
    numerator = numerator.reshape(total_rows, heads_here * HD)
    global_top = lax.pmax(row_top, "blk")
    factor = jnp.exp(row_top - global_top)
    totals = totals * factor
    numerator = (numerator.reshape(total_rows, heads_here, HD) * factor[:, :, None]).reshape(
        total_rows, heads_here * HD
    )
    own_numer = lax.psum_scatter(
        numerator.astype(jnp.bfloat16), "blk", scatter_dimension=1, tiled=True
    ).astype(jnp.float32)
    all_totals = lax.psum(totals, "blk")
    col_width = own_numer.shape[1]
    first_col = lax.axis_index("blk") * col_width
    spread = jnp.repeat(all_totals, HD, axis=1)
    col_totals = lax.dynamic_slice_in_dim(spread, first_col, col_width, 1)
    attended = (own_numer / col_totals).astype(jnp.bfloat16)
    projected = lax.psum_scatter(
        jnp.dot(attended, out_weight, preferred_element_type=jnp.float32),
        ("blk", "rows"),
        scatter_dimension=0,
        tiled=True,
    )
    attn_proj = projected.astype(jnp.bfloat16)
    values_f = attn_proj.astype(jnp.float32)
    mean_square = jnp.mean(values_f * values_f, axis=-1, keepdims=True)
    normed = (values_f * lax.rsqrt(mean_square + EPSILON) * norm_gain.astype(jnp.float32)).astype(
        jnp.bfloat16
    )
    own_tokens = normed.shape[0]
    top_count = expert_ids.shape[1]
    owners = lax.axis_size("blk") * lax.axis_size("rows")
    local_experts = gate_weight.shape[0]
    expert_count = owners * local_experts
    capacity = min(own_tokens, max(2, 2 * top_count * own_tokens // expert_count))
    slot_total = expert_count * capacity
    route_expert = expert_ids.reshape(-1)
    route_count = route_expert.shape[0]
    hits = (route_expert[:, None] == jnp.arange(expert_count, dtype=jnp.int32)[None, :]).astype(
        jnp.int32
    )
    slot_number = jnp.sum(jnp.cumsum(hits, axis=0) * hits, axis=1) - 1
    target = route_expert * capacity + slot_number
    placed = target[:, None] == jnp.arange(slot_total, dtype=jnp.int32)[None, :]
    route_token = jnp.arange(route_count, dtype=jnp.int32) // top_count
    token_pick = route_token[:, None] == jnp.arange(own_tokens, dtype=jnp.int32)[None, :]
    slot_token = jnp.dot(
        placed.astype(jnp.bfloat16).T,
        token_pick.astype(jnp.bfloat16),
        preferred_element_type=jnp.float32,
    ).astype(jnp.bfloat16)
    outgoing = jnp.dot(slot_token, normed, preferred_element_type=jnp.float32).astype(jnp.bfloat16)
    outgoing = outgoing.reshape(owners, local_experts, capacity, -1)
    gate_values = gate_fixed.astype(jnp.float32)
    route_weight = (gate_values / jnp.sum(gate_values, axis=1, keepdims=True)).reshape(-1)
    weighted_pick = token_pick.astype(jnp.float32) * route_weight[:, None]
    blend = jnp.dot(weighted_pick.T, placed.astype(jnp.float32), precision=lax.Precision.HIGHEST)
    finished = run_experts(
        lax.all_to_all(outgoing, ("blk", "rows"), split_axis=0, concat_axis=0, tiled=True),
        gate_weight,
        up_weight,
        down_weight,
    )
    returned = lax.all_to_all(finished, ("blk", "rows"), split_axis=0, concat_axis=0, tiled=True)
    returned_flat = returned.reshape(slot_total, -1)
    mixed = jnp.dot(blend, returned_flat.astype(jnp.float32), precision=lax.Precision.HIGHEST)
    expert_out = mixed.astype(jnp.bfloat16)
    return (attn_proj, expert_out)


def far_of(step, blk):
    return [(at, ((at // 2) ^ step) * 2 + at % 2) for at in range(blk)]


def side_of(size):
    return [(at, at ^ 1) for at in range(size)]


def place_of():
    blk_at = lax.axis_index("blk")
    return blk_at // 2, blk_at % 2


def grant(mebibytes):
    return pltpu.CompilerParams(vmem_limit_bytes=mebibytes << 20)


def in_vmem(count):
    return [pl.BlockSpec(memory_space=pltpu.VMEM)] * count


def prepare_kernel(sizes, *refs):
    far_count, span_length = sizes
    sources, (starts_hbm, ids_hbm, gates_hbm) = refs[:4], refs[4:7]
    targets, (pos_all, routes) = refs[7:11], refs[11:13]
    starts, ids_ref, gates_ref, sems = refs[13:]
    copies = [
        pltpu.make_async_copy(source, target, sems.at[at])
        for at, (source, target) in enumerate(
            zip((starts_hbm, ids_hbm, gates_hbm) + sources, (starts, ids_ref, gates_ref) + targets)
        )
    ]
    for copy in copies:
        copy.start()
    for copy in copies[:3]:
        copy.wait()
    _, near = place_of()
    tokens = pos_all.shape[0]
    piece = tokens // far_count
    for source in range(far_count):
        first = (source * 2 + near) * piece
        base = starts[first // span_length] + first % span_length
        pos_all[source * piece : (source + 1) * piece, :] = base + lax.broadcasted_iota(
            jnp.int32, (piece, HD), 0
        )
    gate_values = gates_ref[...].astype(jnp.float32)
    ids = ids_ref[...]
    route_weight = gate_values / jnp.sum(gate_values, axis=1, keepdims=True)
    own_tokens, top_count = gate_values.shape
    expert_lane = lax.broadcasted_iota(jnp.int32, (own_tokens, HD), 1) - HD // 2
    weight_of = jnp.zeros((own_tokens, HD), jnp.float32)
    for k in range(top_count):
        weight_of += jnp.where(expert_lane == ids[:, k : k + 1], route_weight[:, k : k + 1], 0.0)
    high = weight_of.astype(jnp.bfloat16).astype(jnp.float32)
    routes[...] = jnp.concatenate(
        [high, weight_of - high, jnp.zeros((tokens - 2 * own_tokens, HD), jnp.float32)], axis=0
    )
    for copy in copies[3:]:
        copy.wait()


def fetch_kernel(*refs):
    count = len(refs) // 2
    sems = refs[-1]
    copies = [
        pltpu.make_async_copy(refs[at], refs[count + at], sems.at[at]) for at in range(count)
    ]
    for copy in copies:
        copy.start()
    for copy in copies:
        copy.wait()


def attend_kernel(sizes, *refs):
    far_count, cache_rows, heads = sizes
    q_refs = refs[:far_count]
    key_own, key_side, value_own, value_side, pos_all, routes_ref = refs[far_count : far_count + 6]
    outs = refs[far_count + 6 : 2 * far_count + 6]
    q_all, keys, values, staged = refs[2 * far_count + 6 :]
    far, near = place_of()
    piece = q_refs[0].shape[0]
    tokens = far_count * piece
    own_heads = heads // far_count
    for step in range(far_count):
        source = far ^ step
        row = pl.multiple_of(source * piece, piece)
        for head in range(heads):
            q_all[pl.ds(head * tokens + row, piece), :] = q_refs[step][:, head * HD : (head + 1) * HD]
    keys[:cache_rows, :] = key_own[...]
    keys[cache_rows:, :] = key_side[...]
    values[:cache_rows, :] = value_own[...]
    values[cache_rows:, :] = value_side[...]
    lane_at = lax.broadcasted_iota(jnp.int32, (1, 2 * cache_rows), 1)
    own_first = (far * 2 + near) * cache_rows
    side_first = (far * 2 + 1 - near) * cache_rows - cache_rows
    key_pos = lane_at + jnp.where(lane_at < cache_rows, own_first, side_first)
    visible = key_pos <= pos_all[:, :1]
    routes = routes_ref[...]
    lane = lax.broadcasted_iota(jnp.int32, (tokens, HD), 1)
    scale = 1.0 / math.sqrt(HD)
    joined = 2
    for first in range(0, far_count, joined):
        rows = first * own_heads * tokens
        scores = lax.dot_general(
            q_all[rows : rows + joined * own_heads * tokens, :],
            keys[...],
            (((1,), (1,)), ((), ())),
            preferred_element_type=jnp.float32,
        )
        weights_16 = []
        for group in range(first, first + joined):
            extra = routes
            for j in range(own_heads):
                at = (group - first) * own_heads + j
                part = scores[at * tokens : (at + 1) * tokens] * scale
                part = jnp.where(visible, part, NEG_FILL)
                top = jnp.maximum(jnp.max(part, axis=1, keepdims=True), NEG_FILL / 10)
                top = top.astype(jnp.bfloat16).astype(jnp.float32)
                weights = jnp.exp(part - top)
                total = jnp.sum(weights, axis=1, keepdims=True)
                total_high = total.astype(jnp.bfloat16).astype(jnp.float32)
                extra = jnp.where(lane == 3 * j, top, extra)
                extra = jnp.where(lane == 3 * j + 1, total_high, extra)
                extra = jnp.where(lane == 3 * j + 2, total - total_high, extra)
                weights_16.append(weights.astype(jnp.bfloat16))
            staged[group, :, own_heads * HD :] = extra.astype(jnp.bfloat16)
        numerator = jnp.dot(
            jnp.concatenate(weights_16, axis=0), values[...], preferred_element_type=jnp.float32
        ).astype(jnp.bfloat16)
        for group in range(first, first + joined):
            for j in range(own_heads):
                at = (group - first) * own_heads + j
                staged[group, :, j * HD : (j + 1) * HD] = numerator[at * tokens : (at + 1) * tokens]
    for step in range(far_count):
        outs[step][...] = staged[far ^ step]


def merge_kernel(sizes, *refs):
    far_count, own_heads, own_tokens = sizes
    messages = refs[:far_count]
    weight_own, side, routes, partial = refs[far_count:]
    _, near = place_of()
    tokens = messages[0].shape[0]
    attended = []
    extras = [m[:, own_heads * HD :].astype(jnp.float32) for m in messages]
    for j in range(own_heads):
        tops = [e[:, 3 * j : 3 * j + 1] for e in extras]
        best = tops[0]
        for top in tops[1:]:
            best = jnp.maximum(best, top)
        above = jnp.zeros((tokens, HD), jnp.float32)
        below = jnp.zeros((tokens, 1), jnp.float32)
        for top, e, m in zip(tops, extras, messages):
            factor = jnp.exp(top - best)
            above += factor * m[:, j * HD : (j + 1) * HD].astype(jnp.float32)
            below += factor * (e[:, 3 * j + 1 : 3 * j + 2] + e[:, 3 * j + 2 : 3 * j + 3])
        attended.append(above / below)
    first = jnp.where(near == 0, attended[0], attended[1]).astype(jnp.bfloat16)
    side[...] = jnp.where(near == 0, attended[1], attended[0]).astype(jnp.bfloat16)
    partial[...] = jnp.dot(first, weight_own[...], preferred_element_type=jnp.float32)
    for at, step in enumerate(range(0, far_count, 2)):
        e = extras[step]
        routes[at * own_tokens : (at + 1) * own_tokens, :] = (
            e[:own_tokens] + e[own_tokens : 2 * own_tokens]
        )


def project_kernel(sizes, side, weight_side, merged, keep, send, partial):
    far_count, own_tokens = sizes
    far = place_of()[0]
    row_at = lax.axis_index("rows")
    tokens = side.shape[0]
    partial[...] = merged[...] + jnp.dot(
        side[...], weight_side[...], preferred_element_type=jnp.float32
    )
    piece = tokens // far_count
    other = 1 - row_at
    mine, theirs = [], []
    for step in range(far_count):
        at = pl.multiple_of((far ^ step) * piece + row_at * own_tokens, own_tokens)
        mine.append(partial[pl.ds(at, own_tokens), :])
        at = pl.multiple_of((far ^ step) * piece + other * own_tokens, own_tokens)
        theirs.append(partial[pl.ds(at, own_tokens), :])
    keep[...] = jnp.concatenate(mine, axis=0)
    send[...] = jnp.concatenate(theirs, axis=0).astype(jnp.bfloat16)


def parts_kernel(keep, received, *outs):
    far_count = len(outs)
    own_tokens = keep.shape[0] // far_count
    total = keep[...] + received[...].astype(jnp.float32)
    blocks = [total[at * own_tokens : (at + 1) * own_tokens] for at in range(far_count)]
    for step, out in enumerate(outs):
        taken = [blocks[step ^ even] for even in range(0, far_count, 2)]
        out[...] = jnp.concatenate(taken, axis=0).astype(out.dtype)


def norm_kernel(far_count, *refs):
    parts = refs[:far_count]
    gain, routes, own_rows, spread = refs[far_count:]
    width = gain.shape[1]
    total = parts[0][...].astype(jnp.float32)
    for part in parts[1:]:
        total += part[...].astype(jnp.float32)
    rounded = total.astype(jnp.bfloat16)
    values_f = rounded.astype(jnp.float32)
    own_rows[...] = rounded[: own_rows.shape[0]]
    mean_square = jnp.mean(values_f * values_f, axis=1, keepdims=True)
    spread[:, :width] = (
        values_f * lax.rsqrt(mean_square + EPSILON) * gain[...].astype(jnp.float32)
    ).astype(jnp.bfloat16)
    weight_of = routes[...]
    high = weight_of.astype(jnp.bfloat16).astype(jnp.float32)
    low = pltpu.roll(weight_of - high, HD // 2, 1)
    high = pltpu.roll(high, HD // 2, 1)
    lane = lax.broadcasted_iota(jnp.int32, weight_of.shape, 1)
    spread[:, width:] = jnp.where(
        lane < HD // 2, high, pltpu.roll(low, HD // 2, 1)
    ).astype(jnp.bfloat16)


def expert_kernel(width, count, *refs):
    pieces = refs[:count]
    gate, up, down, keep, send, gathered, hidden = refs[count:]
    rows = pieces[0].shape[0]
    for at, piece in enumerate(pieces):
        gathered[at * rows : (at + 1) * rows, :] = piece[:, :width]
    arrived = gathered[...]
    ff = hidden.shape[1]
    chunk = math.gcd(ff, 256)
    for first in range(0, ff, chunk):
        gate_part = jnp.dot(
            arrived, gate[0, :, first : first + chunk], preferred_element_type=jnp.float32
        )
        up_part = jnp.dot(
            arrived, up[0, :, first : first + chunk], preferred_element_type=jnp.float32
        )
        hidden[:, first : first + chunk] = (
            gate_part / (1.0 + jnp.exp(-gate_part)) * up_part
        ).astype(jnp.bfloat16)
    expert = lax.axis_index("blk") * 2 + lax.axis_index("rows")
    lane = lax.broadcasted_iota(jnp.int32, (rows, HD), 1) % (HD // 2)
    shares = []
    for piece in pieces:
        routes = piece[:, width:].astype(jnp.float32)
        shares.append(jnp.sum(jnp.where(lane == expert, routes, 0.0), axis=1, keepdims=True))
    acted = hidden[...]
    for first in range(0, width, 512):
        last = min(first + 512, width)
        result = jnp.dot(acted, down[0, :, first:last], preferred_element_type=jnp.float32)
        result = result.astype(jnp.bfloat16).astype(jnp.float32)
        for at, share in enumerate(shares):
            target = keep if at < count // 2 else send
            half = at % (count // 2)
            target[half * rows : (half + 1) * rows, first:last] = (
                share * result[at * rows : (at + 1) * rows]
            ).astype(jnp.bfloat16)


def add_kernel(*refs):
    terms, out = refs[:-1], refs[-1]
    total = terms[0][...].astype(jnp.float32)
    for term in terms[1:]:
        total += term[...].astype(jnp.float32)
    out[...] = total.astype(out.dtype)


def quarters_kernel(keep, received, *outs):
    rows = outs[0].shape[0]
    for at, out in enumerate(outs):
        part = slice(at * rows, (at + 1) * rows)
        out[...] = (
            keep[part, :].astype(jnp.float32) + received[part, :].astype(jnp.float32)
        ).astype(out.dtype)


def last_kernel(*refs):
    terms, outs = refs[:4], refs[4:]
    rows = outs[0].shape[0]
    total = terms[0][...]
    for term in terms[1:]:
        total += term[...].astype(jnp.float32)
    for at, out in enumerate(outs):
        out[...] = total[at * rows : (at + 1) * rows].astype(out.dtype)


def paired_device(
    queries,
    cache_keys,
    cache_values,
    span_starts,
    out_weight,
    norm_gain,
    expert_ids,
    gate_fixed,
    gate_weight,
    up_weight,
    down_weight,
):
    blk, row_count = lax.axis_size("blk"), lax.axis_size("rows")
    far_count = blk // 2
    piece, query_width = queries.shape
    heads = query_width // HD
    own_heads = heads // far_count
    own_tokens = expert_ids.shape[0]
    tokens = far_count * piece
    held = far_count * own_tokens
    shared = held // 2
    width = out_weight.shape[1]
    cache_rows = cache_keys.shape[0]
    span_length = blk * piece // SPANS
    hidden = gate_weight.shape[2]
    bf16, f32 = jnp.bfloat16, jnp.float32
    shape_of = jax.ShapeDtypeStruct

    def over_far(arrays):
        moved = [arrays[0]]
        for step in range(1, far_count):
            moved.append(lax.ppermute(arrays[step], "blk", far_of(step, blk)))
        return moved

    def in_hbm(arrays):
        return [pltpu.with_memory_space_constraint(a, pltpu.HBM) for a in arrays]

    def fetched(*arrays):
        return pl.pallas_call(
            fetch_kernel,
            out_shape=[shape_of(a.shape, a.dtype) for a in arrays],
            in_specs=[pl.BlockSpec(memory_space=pltpu.HBM)] * len(arrays),
            out_specs=in_vmem(len(arrays)),
            scratch_shapes=[pltpu.SemaphoreType.DMA((len(arrays),))],
            compiler_params=grant(4),
        )(*in_hbm(arrays))

    def added(shape, dtype, *terms):
        return pl.pallas_call(
            add_kernel,
            out_shape=shape_of(shape, dtype),
            in_specs=in_vmem(len(terms)),
            out_specs=pl.BlockSpec(memory_space=pltpu.VMEM),
            compiler_params=grant(4),
            name="added",
        )(*terms)

    def over_close(arrays):
        moved = [arrays[0]]
        for step in range(1, 4):
            pairs = [(source, source ^ step) for source in range(blk)]
            moved.append(lax.ppermute(arrays[step], "blk", pairs))
        return moved

    def over_near(array):
        return lax.ppermute(array, "blk", side_of(blk))

    def over_rows(array):
        return lax.ppermute(array, "rows", side_of(row_count))

    key_side = over_near(cache_keys)
    value_side = over_near(cache_values)
    q_pieces = over_far([queries] * far_count)
    weight_side = over_near(out_weight)
    local = [queries, cache_keys, cache_values, out_weight]
    *local, pos_all, routes = pl.pallas_call(
        functools.partial(prepare_kernel, (far_count, span_length)),
        out_shape=[shape_of(a.shape, a.dtype) for a in local]
        + [shape_of((tokens, HD), jnp.int32), shape_of((tokens, HD), f32)],
        in_specs=[pl.BlockSpec(memory_space=pltpu.HBM)] * 7,
        out_specs=in_vmem(6),
        scratch_shapes=[
            pltpu.SMEM(span_starts.shape, jnp.int32),
            pltpu.VMEM(expert_ids.shape, jnp.int32),
            pltpu.VMEM(gate_fixed.shape, jnp.int32),
            pltpu.SemaphoreType.DMA((7,)),
        ],
        compiler_params=grant(4),
        name="prepare",
    )(*in_hbm(local + [span_starts, expert_ids, gate_fixed]))
    queries_own, keys_own, values_own, weight_own = local
    q_pieces[0] = queries_own
    message_width = (own_heads + 1) * HD
    messages = pl.pallas_call(
        functools.partial(attend_kernel, (far_count, cache_rows, heads)),
        out_shape=[shape_of((tokens, message_width), bf16)] * far_count,
        in_specs=in_vmem(far_count + 6),
        out_specs=in_vmem(far_count),
        scratch_shapes=[
            pltpu.VMEM((heads * tokens, HD), bf16),
            pltpu.VMEM((2 * cache_rows, HD), bf16),
            pltpu.VMEM((2 * cache_rows, HD), bf16),
            pltpu.VMEM((far_count, tokens, message_width), bf16),
        ],
        compiler_params=grant(12),
        name="attend",
    )(*q_pieces, keys_own, key_side, values_own, value_side, pos_all, routes)
    messages = over_far(messages)
    (down_weight,) = fetched(down_weight)
    side, routes, merged = pl.pallas_call(
        functools.partial(merge_kernel, (far_count, own_heads, own_tokens)),
        out_shape=[shape_of((tokens, HD), bf16), shape_of((shared, HD), f32), shape_of((tokens, width), f32)],
        in_specs=in_vmem(far_count + 1),
        out_specs=in_vmem(3),
        compiler_params=grant(4),
        name="merge",
    )(*messages, weight_own)
    keep, send = pl.pallas_call(
        functools.partial(project_kernel, (far_count, own_tokens)),
        out_shape=[shape_of((held, width), f32), shape_of((held, width), bf16)],
        in_specs=in_vmem(3),
        out_specs=in_vmem(2),
        scratch_shapes=[pltpu.VMEM((tokens, width), f32)],
        compiler_params=grant(6),
        name="project",
    )(side, weight_side, merged)
    parts = pl.pallas_call(
        parts_kernel,
        out_shape=[shape_of((shared, width), f32)] + [shape_of((shared, width), bf16)] * (far_count - 1),
        in_specs=in_vmem(2),
        out_specs=in_vmem(far_count),
        compiler_params=grant(4),
        name="parts",
    )(keep, over_rows(send))
    parts = over_far(parts)
    gate_weight, up_weight = fetched(gate_weight, up_weight)
    attn_proj, normed = pl.pallas_call(
        functools.partial(norm_kernel, far_count),
        out_shape=[pltpu.VMEM((own_tokens, width), bf16), shape_of((shared, width + HD), bf16)],
        in_specs=in_vmem(far_count + 2),
        out_specs=in_vmem(2),
        compiler_params=grant(4),
        name="norm",
    )(*parts, norm_gain.reshape(1, width), routes)
    pieces = over_close([normed] * 4)
    attn_proj = pl.pallas_call(
        add_kernel,
        out_shape=shape_of((own_tokens, width), bf16),
        in_specs=in_vmem(1),
        out_specs=pl.BlockSpec(memory_space=pltpu.VMEM),
        compiler_params=grant(4),
        name="emit",
    )(attn_proj)
    pieces = pieces + [over_rows(piece) for piece in pieces]
    keep, send = pl.pallas_call(
        functools.partial(expert_kernel, width, len(pieces)),
        out_shape=[shape_of((4 * shared, width), bf16)] * 2,
        in_specs=in_vmem(len(pieces) + 3),
        out_specs=in_vmem(2),
        scratch_shapes=[
            pltpu.VMEM((len(pieces) * shared, width), bf16),
            pltpu.VMEM((len(pieces) * shared, hidden), bf16),
        ],
        compiler_params=grant(8),
        name="experts",
    )(*pieces, gate_weight, up_weight, down_weight)
    shares = pl.pallas_call(
        quarters_kernel,
        out_shape=[shape_of((shared, width), f32)] + [shape_of((shared, width), bf16)] * 3,
        in_specs=in_vmem(2),
        out_specs=in_vmem(4),
        compiler_params=grant(4),
        name="quarters",
    )(keep, over_rows(send))
    shares = over_close(shares)
    evens = list(range(0, far_count, 2))
    last = pl.pallas_call(
        last_kernel,
        out_shape=[shape_of((own_tokens, width), f32)]
        + [shape_of((own_tokens, width), bf16)] * (len(evens) - 1),
        in_specs=in_vmem(4),
        out_specs=in_vmem(len(evens)),
        compiler_params=grant(4),
        name="last",
    )(*shares)
    last = [last[0]] + [
        lax.ppermute(term, "blk", far_of(step, blk)) for term, step in zip(last[1:], evens[1:])
    ]
    return (attn_proj, added((own_tokens, width), bf16, *last))


def fits_pairs(mesh, queries, cache_keys, out_weight, expert_ids, gate_weight):
    blk, row_count = mesh.shape["blk"], mesh.shape["rows"]
    parts = mesh.shape["groups"]
    far_count = blk // 2
    if blk % 2 or row_count != 2 or far_count < 2 or far_count & (far_count - 1):
        return False
    heads = queries.shape[1] // (row_count * HD)
    piece = queries.shape[0] // (parts * blk)
    own_tokens = expert_ids.shape[0] // (parts * blk * row_count)
    experts = gate_weight.shape[0]
    return (
        cache_keys.shape[1] == row_count * HD
        and heads == 2 * far_count
        and out_weight.shape[0] == row_count * blk * HD
        and out_weight.shape[1] % HD == 0
        and piece == 2 * own_tokens
        and own_tokens % 8 == 0
        and (blk * piece // SPANS) % piece == 0
        and experts == blk * row_count
        and experts <= HD // 2
        and gate_weight.shape[2] % 128 == 0
    )


def solution(mesh):
    in_specs = (
        P(("groups", "blk"), "rows"),
        P(("groups", "blk"), "rows"),
        P(("groups", "blk"), "rows"),
        P("groups"),
        P(("rows", "blk"), None),
        P(),
        P(("groups", "blk", "rows"), None),
        P(("groups", "blk", "rows"), None),
        P(("blk", "rows"), None, None),
        P(("blk", "rows"), None, None),
        P(("blk", "rows"), None, None),
    )
    out_specs = (P(("groups", "blk", "rows"), None), P(("groups", "blk", "rows"), None))

    def mapped(body):
        return jax.shard_map(
            body, mesh=mesh, in_specs=in_specs, out_specs=out_specs, check_vma=False
        )

    def run(*arrays):
        queries, cache_keys, out_weight = arrays[0], arrays[1], arrays[4]
        expert_ids, gate_weight = arrays[6], arrays[8]
        if not fits_pairs(mesh, queries, cache_keys, out_weight, expert_ids, gate_weight):
            return mapped(on_device)(*arrays)
        return mapped(paired_device)(*arrays)

    return run
```
